128 devices in a mesh: replica: 8 (over x, y_hi), fsdp: 16 (over y_lo, z, core).
Axes of the slice: x: 4, y: 4 (y_hi: 2, y_lo: 2; y = y_hi * 2 + y_lo), z: 4, core: 2. Of those that a mesh axis runs over, the one named last changes fastest.
Arguments:
- tokens: bfloat16 [147456, 1024], P(('replica', 'fsdp')), may hold values from -6 to 6
- cotangent: bfloat16 [147456, 1024], P(('replica', 'fsdp')), may hold values from -6 to 6
- lengths: int32 [128, 3], P(('replica', 'fsdp')), may hold values from 1 to 1024, 1152 in all within a row
- deal_order: int32 [147456], P(('replica', 'fsdp')), may hold values from 0 to 147455, as said below
- inverse: int32 [147456], P(('replica', 'fsdp')), may hold values from 0 to 147455, as said below
- ln1_gain: bfloat16 [1024], P('fsdp'), may hold values from 0.5 to 1.5
- ln1_bias: bfloat16 [1024], P('fsdp'), may hold values from -1 to 1
- w_qkv: bfloat16 [1024, 3072], P('fsdp'), may hold values from -0.1875 to 0.1875
- b_query: bfloat16 [1024], P('fsdp'), may hold values from -1 to 1
- b_value: bfloat16 [1024], P('fsdp'), may hold values from -1 to 1
- head_scale: bfloat16 [16], P('fsdp'), may hold values from 0.5 to 1.5
- w_out: bfloat16 [1024, 1024], P('fsdp'), may hold values from -0.1875 to 0.1875
- b_out: bfloat16 [1024], P('fsdp'), may hold values from -1 to 1
- post_gain: bfloat16 [1024], P('fsdp'), may hold values from 0.5 to 1.5
- post_bias: bfloat16 [1024], P('fsdp'), may hold values from -1 to 1
- ln2_gain: bfloat16 [1024], P('fsdp'), may hold values from 0.5 to 1.5
- ln2_bias: bfloat16 [1024], P('fsdp'), may hold values from -1 to 1
- w_fc1: bfloat16 [1024, 4096], P('fsdp'), may hold values from -0.1875 to 0.1875
- b_fc1: bfloat16 [4096], P('fsdp'), may hold values from -1 to 1
- ffn_gain: bfloat16 [4096], P('fsdp'), may hold values from 0.5 to 1.5
- ffn_bias: bfloat16 [4096], P('fsdp'), may hold values from -1 to 1
- w_fc2: bfloat16 [4096, 1024], P('fsdp'), may hold values from -0.09375 to 0.09375
- b_fc2: bfloat16 [1024], P('fsdp'), may hold values from -1 to 1
Outputs:
- output: bfloat16 [147456, 1024], P(('replica', 'fsdp'))
- grad_tokens: bfloat16 [147456, 1024], P(('replica', 'fsdp'))
- grad_ln1_gain: float32 [1024], P('fsdp')
- grad_ln1_bias: float32 [1024], P('fsdp')
- grad_w_qkv: float32 [1024, 3072], P('fsdp')
- grad_b_query: float32 [1024], P('fsdp')
- grad_b_value: float32 [1024], P('fsdp')
- grad_head_scale: float32 [16], P('fsdp')
- grad_w_out: float32 [1024, 1024], P('fsdp')
- grad_b_out: float32 [1024], P('fsdp')
- grad_post_gain: float32 [1024], P('fsdp')
- grad_post_bias: float32 [1024], P('fsdp')
- grad_ln2_gain: float32 [1024], P('fsdp')
- grad_ln2_bias: float32 [1024], P('fsdp')
- grad_w_fc1: float32 [1024, 4096], P('fsdp')
- grad_b_fc1: float32 [4096], P('fsdp')
- grad_ffn_gain: float32 [4096], P('fsdp')
- grad_ffn_bias: float32 [4096], P('fsdp')
- grad_w_fc2: float32 [4096, 1024], P('fsdp')
- grad_b_fc2: float32 [1024], P('fsdp')
The draws below stay inside these ranges and needn't reach their ends.
Inputs may be any that keep to these rules, and one draw needn't show every extreme that they name: deal_order is a permutation of all rows; of the 1152 rows that one device holds in the device order exactly 9 come from each device's rows of the given order. inverse[deal_order[i]] = i for every i. `lengths`: each row sums to 1152; each row's longest sequence has 1024 rows.
All inputs are finite; a program needn't handle non-finite values.
Results may differ from the reference program's by a relative error of at most 0.03.
Values may be sent and summed in bfloat16 or wider, within the bound.
No kernel may reach another device: no remote copies, remote signals or barrier semaphores. Data moves between devices by JAX's collectives and lax.ppermute only.
A program may use at most 320 MiB of HBM per device.

```python
import math
import jax
import jax.numpy as jnp
import numpy as np
from jax import lax

D = 1024
FF = 4096
H = 16
HD = 64
TOK_DEV = 1152
SEQ_DEV = 3
MAXLEN = 1024
QB = 576
TOKENS = 147456
N_REPLICA = 8
N_FSDP = 16


def dealing(base_key):
    devices = N_REPLICA * N_FSDP
    per_pair = TOK_DEV // devices
    inner_key = jax.random.fold_in(base_key, 7)
    key_rows, key_source, key_local = jax.random.split(inner_key, 3)
    shuffle_rows = jax.vmap(lambda subkey: jax.random.permutation(subkey, TOK_DEV))(jax.random.split(key_rows, devices))
    source_order = jax.vmap(lambda subkey: jax.random.permutation(subkey, devices))(jax.random.split(key_source, devices))
    local_order = jax.vmap(lambda subkey: jax.random.permutation(subkey, TOK_DEV))(jax.random.split(key_local, devices))
    source = jnp.take_along_axis(source_order, shuffle_rows // per_pair, axis=1)
    slot_index = jnp.arange(devices, dtype=jnp.int32)[:, None] * per_pair + shuffle_rows % per_pair
    local_row = local_order[source, slot_index]
    return (source * TOK_DEV + local_row).reshape(-1).astype(jnp.int32)


def draw_deal_order(key, part):
    return dealing(key)


def draw_inverse(key, part):
    return jnp.argsort(dealing(key), stable=True).astype(jnp.int32)


def shard_levels(rng, shape, pieces, smallest, largest):
    gain, own = 1.0, jax.random.fold_in(rng, 6)
    for position, parts in pieces:
        draws = jnp.exp(jax.random.uniform(jax.random.fold_in(own, position), (parts,), jnp.float32, smallest / len(pieces), largest / len(pieces)))
        gain = gain * jnp.repeat(draws, shape[position] // parts).reshape([-1 if axis == position else 1 for axis in range(len(shape))])
    return gain


def length_profile(number_of, total, reach, lean):
    portions = [(1 << 20) // math.isqrt(rank ** lean) + 1 for rank in range(2, number_of + 1)]
    spare, counts = total - reach - (number_of - 1), [1] * (number_of - 1)
    while spare > 0:
        movable = [i for i in range(number_of - 1) if counts[i] < reach]
        mass, remaining = sum([portions[i] for i in movable]), spare
        for i in movable:
            more = min(reach - counts[i], max(1, remaining * portions[i] // mass), spare)
            counts[i] = counts[i] + more
            spare = spare - more
    return np.array([reach] + counts)


def ragged(key, count, total, bound, lean):
    if count == 2:
        one = jax.random.randint(key, (), max(1, total - bound), min(bound, total - 1) + 1)
        return jnp.stack([one, total - one])
    sizes = jnp.asarray(length_profile(count, total, bound, lean), jnp.int32)
    couples = (count - 1) // 2
    source_of, receiver = sizes[1:1 + 2 * couples:2], sizes[2:2 + 2 * couples:2]
    slack = jnp.minimum(source_of - 1, bound - receiver)
    shifted = jax.random.randint(jax.random.fold_in(key, 1), (couples,), 0, 1 << 20) % (slack + 1)
    sizes = sizes.at[1:1 + 2 * couples:2].set(source_of - shifted).at[2:2 + 2 * couples:2].set(receiver + shifted)
    return sizes[jax.random.permutation(jax.random.fold_in(key, 2), count)]


def bell_draw(rng, shape, deviation, bound, cuts=(), kind=jnp.bfloat16):
    array = jax.random.normal(rng, shape, jnp.float32) * deviation
    if len(cuts) > 0:
        array = shard_levels(rng, shape, cuts, -0.22, 0.18) * array
    return jnp.clip(array, min=-bound, max=bound).astype(kind)


def setup_inputs(seed: int = 0) -> dict:
    key_list = jax.random.split(jax.random.key(seed), 24)
    tokens = bell_draw(key_list[0], (TOKENS, D), 1.0, 6.0, ((0, 128),))
    cotangent = bell_draw(key_list[1], (TOKENS, D), 1.0, 6.0, ((0, 128),))
    lengths = jax.vmap(lambda own: ragged(own, SEQ_DEV, TOK_DEV, MAXLEN, 2))(jax.random.split(key_list[2], (N_REPLICA * N_FSDP))).reshape((N_REPLICA * N_FSDP, SEQ_DEV)).astype(jnp.int32)
    deal_order = draw_deal_order(jax.random.fold_in(key_list[23], 71), 0)
    inverse = draw_inverse(jax.random.fold_in(key_list[23], 71), 0)
    ln1_gain = jnp.clip(1.0 + 0.1 * jax.random.normal(key_list[5], (D,), jnp.float32), 0.5, 1.5).astype(jnp.bfloat16)
    ln1_bias = bell_draw(key_list[6], (D,), 0.2, 1.0, ((0, 16),))
    w_qkv = bell_draw(key_list[7], (D, 3 * D), D ** -0.5, 0.1875, ((0, 16),))
    b_query = bell_draw(key_list[8], (D,), 0.2, 1.0, ((0, 16),))
    b_value = bell_draw(key_list[9], (D,), 0.2, 1.0, ((0, 16),))
    head_scale = jnp.clip(0.5 + 1.0 * jax.random.uniform(key_list[10], (H,), jnp.float32) ** shard_levels(key_list[10], (H,), ((0, 16),), -0.2, 0.2), 0.5, 1.5).astype(jnp.bfloat16)
    w_out = bell_draw(key_list[11], (D, D), D ** -0.5, 0.1875, ((0, 16),))
    b_out = bell_draw(key_list[12], (D,), 0.2, 1.0, ((0, 16),))
    post_gain = jnp.clip(1.0 + 0.1 * jax.random.normal(key_list[13], (D,), jnp.float32), 0.5, 1.5).astype(jnp.bfloat16)
    post_bias = bell_draw(key_list[14], (D,), 0.2, 1.0, ((0, 16),))
    ln2_gain = jnp.clip(1.0 + 0.1 * jax.random.normal(key_list[15], (D,), jnp.float32), 0.5, 1.5).astype(jnp.bfloat16)
    ln2_bias = bell_draw(key_list[16], (D,), 0.2, 1.0, ((0, 16),))
    w_fc1 = bell_draw(key_list[17], (D, FF), D ** -0.5, 0.1875, ((0, 16),))
    b_fc1 = bell_draw(key_list[18], (FF,), 0.2, 1.0, ((0, 16),))
    ffn_gain = jnp.clip(1.0 + 0.1 * jax.random.normal(key_list[19], (FF,), jnp.float32), 0.5, 1.5).astype(jnp.bfloat16)
    ffn_bias = bell_draw(key_list[20], (FF,), 0.2, 1.0, ((0, 16),))
    w_fc2 = bell_draw(key_list[21], (FF, D), FF ** -0.5, 0.09375, ((0, 16),))
    b_fc2 = bell_draw(key_list[22], (D,), 0.2, 1.0, ((0, 16),))
    return {"tokens": tokens, "cotangent": cotangent, "lengths": lengths, "deal_order": deal_order, "inverse": inverse, "ln1_gain": ln1_gain, "ln1_bias": ln1_bias, "w_qkv": w_qkv, "b_query": b_query, "b_value": b_value, "head_scale": head_scale, "w_out": w_out, "b_out": b_out, "post_gain": post_gain, "post_bias": post_bias, "ln2_gain": ln2_gain, "ln2_bias": ln2_bias, "w_fc1": w_fc1, "b_fc1": b_fc1, "ffn_gain": ffn_gain, "ffn_bias": ffn_bias, "w_fc2": w_fc2, "b_fc2": b_fc2}


EPS = 1e-05
NEG = -1000000000.0

@jax.custom_vjp
def low(v):
    return lax.optimization_barrier(v.astype(jnp.bfloat16)).astype(jnp.float32)

@jax.custom_vjp
def low_back(v):
    return v

def low_keep(v):
    return (low(v), None)

def low_pass(kept, grad):
    return (grad,)

def back_keep(v):
    return (v, None)

def back_low(kept, grad):
    return (low(grad),)
low.defvjp(low_keep, low_pass)
low_back.defvjp(back_keep, back_low)

def layer_norm(values, gain_vec, bias_vec):
    mean_row = lax.optimization_barrier(jnp.mean(values, axis=-1, keepdims=True))
    centred = values - mean_row
    spread = lax.optimization_barrier(jnp.mean(centred * centred, axis=-1, keepdims=True))
    return centred * lax.rsqrt(spread + EPS) * gain_vec + bias_vec

def both_ways(values):
    return low_back(low(values))

def matmul(left, right):
    return jnp.dot(left, right, precision=lax.Precision.HIGHEST)

def segment_ids(lengths_row):
    seq_ends = jnp.cumsum(lengths_row).astype(jnp.int32)
    places = jnp.arange(TOK_DEV, dtype=jnp.int32)
    return lax.optimization_barrier(jnp.sum((places[:, None] >= seq_ends[None, :]).astype(jnp.int32), axis=1)).astype(jnp.int32)

def attend(query, key_all, value_all, segments):
    scale_val = HD ** (-0.5)
    q_heads = query.reshape(TOK_DEV, H, HD)
    k_heads = key_all.reshape(TOK_DEV, H, HD)
    v_heads = value_all.reshape(TOK_DEV, H, HD)
    places = jnp.arange(TOK_DEV, dtype=jnp.int32)

    def one_block(q_start):
        q_rows = lax.dynamic_slice_in_dim(q_heads, q_start, QB, 0)
        q_pos = q_start + jnp.arange(QB, dtype=jnp.int32)
        q_seg = lax.dynamic_slice_in_dim(segments, q_start, QB, 0)
        allowed = (q_seg[:, None] == segments[None, :]) & (places[None, :] <= q_pos[:, None])
        raw_scores = jnp.einsum('qhd,khd->hqk', q_rows, k_heads, precision=lax.Precision.HIGHEST) * scale_val
        scores = low_back(jnp.where(allowed[None], raw_scores, NEG))
        row_max = lax.optimization_barrier(jnp.max(scores, axis=-1, keepdims=True))
        exponent = jnp.exp(scores - row_max)
        prob_rows = exponent / lax.optimization_barrier(jnp.sum(exponent, axis=-1, keepdims=True))
        mixed_rows = jnp.einsum('hqk,khd->qhd', low(prob_rows), v_heads, precision=lax.Precision.HIGHEST)
        return mixed_rows.reshape(QB, D)
    starts = (jnp.arange(TOK_DEV // QB, dtype=jnp.int32) * QB).astype(jnp.int32)
    return lax.map(jax.checkpoint(one_block), starts).reshape(TOK_DEV, D)

def layer(x_vals, params, segments):
    g_one, b_one, w_qkv, b_query, b_value, head_scale, w_out, b_out, post_gain, post_bias, g_two, b_two, w_fc1, b_fc1, ffn_gain, ffn_bias, w_fc2, b_fc2 = params
    normed = low(layer_norm(x_vals, g_one, b_one))
    bias_full = jnp.concatenate([b_query, jnp.zeros((D,), jnp.float32), b_value])
    proj = both_ways(matmul(normed, w_qkv) + bias_full)
    attn = attend(proj[:, :D], proj[:, D:2 * D], proj[:, 2 * D:], segments)
    mixed = low(low_back(attn) * jnp.repeat(head_scale, HD))
    z_vals = low_back(matmul(mixed, w_out) + b_out)
    resid = x_vals + layer_norm(z_vals, post_gain, post_bias)
    normed_two = low(layer_norm(resid, g_two, b_two))
    up_vals = low_back(matmul(normed_two, w_fc1) + b_fc1)
    inner = low(layer_norm(jax.nn.gelu(up_vals, approximate=False), ffn_gain, ffn_bias))
    branch = low_back(matmul(inner, w_fc2) + b_fc2)
    return resid + branch

def reference(tokens, cotangent, lengths, deal_order, inverse, ln1_gain, ln1_bias, w_qkv, b_query, b_value, head_scale, w_out, b_out, post_gain, post_bias, ln2_gain, ln2_bias, w_fc1, b_fc1, ffn_gain, ffn_bias, w_fc2, b_fc2):
    devices = N_REPLICA * N_FSDP
    params = tuple((weight.astype(jnp.float32) for weight in (ln1_gain, ln1_bias, w_qkv, b_query, b_value, head_scale, w_out, b_out, post_gain, post_bias, ln2_gain, ln2_bias, w_fc1, b_fc1, ffn_gain, ffn_bias, w_fc2, b_fc2)))
    x_blocks = jnp.take(tokens, deal_order, axis=0).reshape(devices, TOK_DEV, D)
    dy_blocks = jnp.take(cotangent, deal_order, axis=0).reshape(devices, TOK_DEV, D)

    def step(totals, item):
        x_block, dy_block, lengths_row = item
        segments = segment_ids(lengths_row)

        def forward(x_inner, param_vals):
            return layer(x_inner, param_vals, segments)
        out_vals, pull = jax.vjp(forward, x_block.astype(jnp.float32), params)
        dx_vals, dparams = pull(dy_block.astype(jnp.float32))
        totals = jax.tree.map(lambda running, extra: running + extra, totals, dparams)
        return (totals, (out_vals.astype(jnp.bfloat16), dx_vals.astype(jnp.bfloat16)))
    start_totals = jax.tree.map(jnp.zeros_like, params)
    totals, (outs, dxs) = lax.scan(step, start_totals, (x_blocks, dy_blocks, lengths))
    output = jnp.take(outs.reshape(TOKENS, D), inverse, axis=0)
    grad_tokens = jnp.take(dxs.reshape(TOKENS, D), inverse, axis=0)
    return (output, grad_tokens, totals[0], totals[1], totals[2], totals[3], totals[4], totals[5], totals[6], totals[7], totals[8], totals[9], totals[10], totals[11], totals[12], totals[13], totals[14], totals[15], totals[16], totals[17])
```

```python
import jax
import jax.numpy as jnp
from jax import lax
from jax.sharding import PartitionSpec as P

H = 16
HD = 64
QB = 576


EPS = 1e-05
NEG = -1000000000.0


def side_by_side(arrays, axis, dim, along):
    columns = [a.reshape(*a.shape[:along], -1) for a in arrays]
    both = jnp.concatenate(columns, axis=along)
    whole, at, gathered = (lax.psum_scatter(both, axis, scatter_dimension=dim, tiled=True), 0, [])
    for a, column in zip(arrays, columns):
        share = whole[..., at : at + column.shape[along]]
        gathered.append(share.reshape(*share.shape[:along], *a.shape[along:]))
        at += column.shape[along]
    return tuple(gathered)


def layer_norm(values, gain_vec, bias_vec):
    mean_row = jnp.mean(values, axis=-1, keepdims=True)
    centred = values - mean_row
    spread = jnp.mean(centred * centred, axis=-1, keepdims=True)
    return centred * lax.rsqrt(spread + EPS) * gain_vec + bias_vec


def gelu_norm(values, gain_vec, bias_vec):
    return layer_norm(jax.nn.gelu(values, approximate=False), gain_vec, bias_vec)


def segment_ids(lengths_row, count):
    places = jnp.arange(count, dtype=jnp.int32)
    segments = jnp.zeros((count,), jnp.int32)
    seq_end = jnp.zeros((), jnp.int32)
    for i in range(lengths_row.shape[0]):
        seq_end = seq_end + lengths_row[i]
        segments = segments + (places >= seq_end).astype(jnp.int32)
    return segments


def block_parts(proj_b, segments, turn_index):
    count = proj_b.shape[0]
    width = H * HD
    group_cols = 4 * HD
    groups = H // 4
    window = min(count, 3 * QB)
    q_start = turn_index // groups * QB
    k_start = jnp.clip(q_start + QB - window, 0, count - window)
    col_start = turn_index % groups * group_cols
    query_rows = lax.dynamic_slice(proj_b, (q_start, col_start), (QB, group_cols)).reshape(
        QB, 4, HD
    )
    key_rows = lax.dynamic_slice(
        proj_b, (k_start, width + col_start), (window, group_cols)
    ).reshape(window, 4, HD)
    value_rows = lax.dynamic_slice(
        proj_b, (k_start, 2 * width + col_start), (window, group_cols)
    ).reshape(window, 4, HD)
    q_seg = lax.dynamic_slice(segments, (q_start,), (QB,))
    q_pos = q_start + jnp.arange(QB, dtype=jnp.int32)
    k_pos = k_start + jnp.arange(window, dtype=jnp.int32)
    allowed = (q_seg[:, None] == segments[None, :]) & (k_pos[None, :] <= q_pos[:, None])
    raw_scores = jnp.einsum(
        "qhd,khd->hqk", query_rows, key_rows, preferred_element_type=jnp.float32
    ) * HD ** (-0.5)
    scores = jnp.where(allowed[None], raw_scores, NEG)
    return (query_rows, key_rows, value_rows, scores, q_start, k_start, col_start)


def attend_forward(proj_b, segments):
    count = proj_b.shape[0]
    turns = count // QB * (H // 4)

    def attend_turn(turn_index, carry):
        attn_acc, lse_acc = carry
        query_rows, key_rows, value_rows, scores, q_start, k_start, col_start = block_parts(
            proj_b, segments, turn_index
        )
        row_max = jnp.max(scores, axis=-1, keepdims=True)
        exponent = jnp.exp(scores - row_max)
        row_total = jnp.sum(exponent, axis=-1, keepdims=True)
        prob_rows = exponent / row_total
        mixed_rows = jnp.einsum(
            "hqk,khd->qhd",
            prob_rows.astype(jnp.bfloat16),
            value_rows,
            preferred_element_type=jnp.float32,
        )
        attn_acc = lax.dynamic_update_slice(
            attn_acc, mixed_rows.reshape(QB, 4 * HD), (q_start, col_start)
        )
        lse_rows = (row_max + jnp.log(row_total))[..., 0]
        head_start = turn_index % (H // 4) * 4
        lse_acc = lax.dynamic_update_slice(lse_acc, lse_rows, (head_start, q_start))
        return (attn_acc, lse_acc)

    initial = (jnp.zeros((count, H * HD), jnp.float32), jnp.zeros((H, count), jnp.float32))
    return lax.fori_loop(0, turns, attend_turn, initial)


def attend_backward(proj_b, segments, lse_all, d_attn_b):
    count = proj_b.shape[0]
    width = H * HD
    window = min(count, 3 * QB)
    turns = count // QB * (H // 4)
    scale_val = HD ** (-0.5)

    def back_turn(turn_index, grad_acc):
        query_rows, key_rows, value_rows, scores, q_start, k_start, col_start = block_parts(
            proj_b, segments, turn_index
        )
        head_start = turn_index % (H // 4) * 4
        lse_rows = lax.dynamic_slice(lse_all, (head_start, q_start), (4, QB))
        prob_rows = jnp.exp(scores - lse_rows[..., None])
        d_out = lax.dynamic_slice(d_attn_b, (q_start, col_start), (QB, 4 * HD)).reshape(QB, 4, HD)
        d_prob = jnp.einsum("qhd,khd->hqk", d_out, value_rows, preferred_element_type=jnp.float32)
        centre = jnp.sum(prob_rows * d_prob, axis=-1, keepdims=True)
        d_score = (prob_rows * (d_prob - centre)).astype(jnp.bfloat16)
        d_query = (
            jnp.einsum("hqk,khd->qhd", d_score, key_rows, preferred_element_type=jnp.float32)
            * scale_val
        )
        d_key = (
            jnp.einsum("hqk,qhd->khd", d_score, query_rows, preferred_element_type=jnp.float32)
            * scale_val
        )
        d_value = jnp.einsum(
            "hqk,qhd->khd",
            prob_rows.astype(jnp.bfloat16),
            d_out,
            preferred_element_type=jnp.float32,
        )
        grad_acc = lax.dynamic_update_slice(
            grad_acc, d_query.reshape(QB, 4 * HD), (q_start, col_start)
        )
        old_key = lax.dynamic_slice(grad_acc, (k_start, width + col_start), (window, 4 * HD))
        grad_acc = lax.dynamic_update_slice(
            grad_acc, old_key + d_key.reshape(window, 4 * HD), (k_start, width + col_start)
        )
        old_value = lax.dynamic_slice(grad_acc, (k_start, 2 * width + col_start), (window, 4 * HD))
        grad_acc = lax.dynamic_update_slice(
            grad_acc, old_value + d_value.reshape(window, 4 * HD), (k_start, 2 * width + col_start)
        )
        return grad_acc

    return lax.fori_loop(0, turns, back_turn, jnp.zeros((count, 3 * width), jnp.float32))


def on_device(
    tokens,
    cotangent,
    lengths,
    deal_order,
    inverse,
    ln1_gain,
    ln1_bias,
    w_qkv,
    b_query,
    b_value,
    head_scale,
    w_out,
    b_out,
    post_gain,
    post_bias,
    ln2_gain,
    ln2_bias,
    w_fc1,
    b_fc1,
    ffn_gain,
    ffn_bias,
    w_fc2,
    b_fc2,
):
    devices = lax.axis_size(("replica", "fsdp"))
    count = tokens.shape[0]
    width = tokens.shape[1]
    per_pair = count // devices
    send_order = jnp.argsort(inverse)
    src_device = deal_order // count
    recv_order = jnp.argsort(src_device * count + jnp.arange(count, dtype=jnp.int32))
    placing = jnp.argsort(recv_order)
    got_x, got_dy = (
        lax.all_to_all(
            jnp.take(tokens, send_order, axis=0).reshape(devices, per_pair, width),
            ("replica", "fsdp"),
            split_axis=0,
            concat_axis=0,
            tiled=True,
        ),
        lax.all_to_all(
            jnp.take(cotangent, send_order, axis=0).reshape(devices, per_pair, width),
            ("replica", "fsdp"),
            split_axis=0,
            concat_axis=0,
            tiled=True,
        ),
    )
    x_rows = jnp.take(got_x.reshape(count, width), placing, axis=0)
    dy_rows = jnp.take(got_dy.reshape(count, width), placing, axis=0)
    segments = segment_ids(lengths[0], count)
    g_one, b_one, qkv_full, bq_full, bv_full, hs_full, out_full, bo_full, pg_full, pb_full = (
        lax.all_gather(ln1_gain, "fsdp", axis=0, tiled=True),
        lax.all_gather(ln1_bias, "fsdp", axis=0, tiled=True),
        lax.all_gather(w_qkv, "fsdp", axis=0, tiled=True),
        lax.all_gather(b_query, "fsdp", axis=0, tiled=True),
        lax.all_gather(b_value, "fsdp", axis=0, tiled=True),
        lax.all_gather(head_scale, "fsdp", axis=0, tiled=True),
        lax.all_gather(w_out, "fsdp", axis=0, tiled=True),
        lax.all_gather(b_out, "fsdp", axis=0, tiled=True),
        lax.all_gather(post_gain, "fsdp", axis=0, tiled=True),
        lax.all_gather(post_bias, "fsdp", axis=0, tiled=True),
    )
    x_vals = x_rows.astype(jnp.float32)
    normed, ln1_pull = jax.vjp(
        layer_norm, x_vals, g_one.astype(jnp.float32), b_one.astype(jnp.float32)
    )
    normed_b = normed.astype(jnp.bfloat16)
    bias_full = jnp.concatenate(
        [bq_full.astype(jnp.float32), jnp.zeros((width,), jnp.float32), bv_full.astype(jnp.float32)]
    )
    proj_b = (jnp.dot(normed_b, qkv_full, preferred_element_type=jnp.float32) + bias_full).astype(
        jnp.bfloat16
    )
    attn, lse_all = attend_forward(proj_b, segments)
    mixed_b = (attn * jnp.repeat(hs_full.astype(jnp.float32), HD)).astype(jnp.bfloat16)
    z_vals = jnp.dot(mixed_b, out_full, preferred_element_type=jnp.float32) + bo_full.astype(
        jnp.float32
    )
    post_vals, post_pull = jax.vjp(
        layer_norm, z_vals, pg_full.astype(jnp.float32), pb_full.astype(jnp.float32)
    )
    resid = x_vals + post_vals
    g_two, b_two, fc1_full, bf1_full, fg_full, fb_full, fc2_full, bf2_full = (
        lax.all_gather(ln2_gain, "fsdp", axis=0, tiled=True),
        lax.all_gather(ln2_bias, "fsdp", axis=0, tiled=True),
        lax.all_gather(w_fc1, "fsdp", axis=0, tiled=True),
        lax.all_gather(b_fc1, "fsdp", axis=0, tiled=True),
        lax.all_gather(ffn_gain, "fsdp", axis=0, tiled=True),
        lax.all_gather(ffn_bias, "fsdp", axis=0, tiled=True),
        lax.all_gather(w_fc2, "fsdp", axis=0, tiled=True),
        lax.all_gather(b_fc2, "fsdp", axis=0, tiled=True),
    )
    normed_two, ln2_pull = jax.vjp(
        layer_norm, resid, g_two.astype(jnp.float32), b_two.astype(jnp.float32)
    )
    normed_two_b = normed_two.astype(jnp.bfloat16)
    up_vals = jnp.dot(normed_two_b, fc1_full, preferred_element_type=jnp.float32) + bf1_full.astype(
        jnp.float32
    )
    inner, inner_pull = jax.vjp(
        gelu_norm, up_vals, fg_full.astype(jnp.float32), fb_full.astype(jnp.float32)
    )
    inner_b = inner.astype(jnp.bfloat16)
    out_rows = (
        resid
        + jnp.dot(inner_b, fc2_full, preferred_element_type=jnp.float32)
        + bf2_full.astype(jnp.float32)
    ).astype(jnp.bfloat16)
    fc1_back, fc2_back = (
        lax.all_gather(w_fc1, "fsdp", axis=0, tiled=True),
        lax.all_gather(w_fc2, "fsdp", axis=0, tiled=True),
    )
    dy_vals = dy_rows.astype(jnp.float32)
    grad_fc2 = jnp.einsum("tf,td->fd", inner_b, dy_rows, preferred_element_type=jnp.float32)
    grad_bf2 = jnp.sum(dy_vals, axis=0)
    d_inner = jnp.einsum("td,fd->tf", dy_rows, fc2_back, preferred_element_type=jnp.float32)
    d_up, grad_fg, grad_fb = inner_pull(d_inner)
    d_up_b = d_up.astype(jnp.bfloat16)
    grad_fc1 = jnp.einsum("td,tf->df", normed_two_b, d_up_b, preferred_element_type=jnp.float32)
    grad_bf1 = jnp.sum(d_up_b.astype(jnp.float32), axis=0)
    d_normed_two = jnp.einsum("tf,df->td", d_up_b, fc1_back, preferred_element_type=jnp.float32)
    d_resid_two, grad_g_two, grad_b_two = ln2_pull(d_normed_two)
    d_resid = dy_vals + d_resid_two
    ffn_grads = (
        lax.psum_scatter(
            grad_g_two.astype(jnp.bfloat16), "fsdp", scatter_dimension=0, tiled=True
        ).astype(jnp.float32),
        *tuple(
            (
                part.astype(jnp.float32)
                for part in side_by_side(
                    (grad_b_two.astype(jnp.bfloat16), grad_fc1.astype(jnp.bfloat16)), "fsdp", 0, 1
                )
            )
        ),
        lax.psum_scatter(
            grad_bf1.astype(jnp.bfloat16), "fsdp", scatter_dimension=0, tiled=True
        ).astype(jnp.float32),
        lax.psum_scatter(
            grad_fg.astype(jnp.bfloat16), "fsdp", scatter_dimension=0, tiled=True
        ).astype(jnp.float32),
        *tuple(
            (
                part.astype(jnp.float32)
                for part in side_by_side(
                    (grad_fb.astype(jnp.bfloat16), grad_fc2.astype(jnp.bfloat16)), "fsdp", 0, 1
                )
            )
        ),
        lax.psum_scatter(
            grad_bf2.astype(jnp.bfloat16), "fsdp", scatter_dimension=0, tiled=True
        ).astype(jnp.float32),
    )
    ffn_grads = (
        lax.psum(ffn_grads[0].astype(jnp.bfloat16), "replica").astype(jnp.float32),
        lax.psum(ffn_grads[1].astype(jnp.bfloat16), "replica").astype(jnp.float32),
        lax.psum(ffn_grads[2].astype(jnp.bfloat16), "replica").astype(jnp.float32),
        lax.psum(ffn_grads[3].astype(jnp.bfloat16), "replica").astype(jnp.float32),
        lax.psum(ffn_grads[4].astype(jnp.bfloat16), "replica").astype(jnp.float32),
        lax.psum(ffn_grads[5].astype(jnp.bfloat16), "replica").astype(jnp.float32),
        lax.psum(ffn_grads[6].astype(jnp.bfloat16), "replica").astype(jnp.float32),
        lax.psum(ffn_grads[7].astype(jnp.bfloat16), "replica").astype(jnp.float32),
    )
    qkv_back, out_back, hs_back = (
        lax.all_gather(w_qkv, "fsdp", axis=0, tiled=True),
        lax.all_gather(w_out, "fsdp", axis=0, tiled=True),
        lax.all_gather(head_scale, "fsdp", axis=0, tiled=True),
    )
    d_z, grad_pg, grad_pb = post_pull(d_resid)
    d_z_b = d_z.astype(jnp.bfloat16)
    grad_out = jnp.einsum("te,td->ed", mixed_b, d_z_b, preferred_element_type=jnp.float32)
    grad_bo = jnp.sum(d_z_b.astype(jnp.float32), axis=0)
    d_mixed = jnp.einsum("td,ed->te", d_z_b, out_back, preferred_element_type=jnp.float32)
    grad_hs = jnp.sum(jnp.sum(d_mixed * attn, axis=0).reshape(H, HD), axis=1)
    d_attn_b = (d_mixed * jnp.repeat(hs_back.astype(jnp.float32), HD)).astype(jnp.bfloat16)
    d_proj_b = attend_backward(proj_b, segments, lse_all, d_attn_b).astype(jnp.bfloat16)
    grad_qkv = jnp.einsum("td,te->de", normed_b, d_proj_b, preferred_element_type=jnp.float32)
    col_sums = jnp.sum(d_proj_b.astype(jnp.float32), axis=0)
    grad_bq = col_sums[:width]
    grad_bv = col_sums[2 * width :]
    d_normed = jnp.einsum("te,de->td", d_proj_b, qkv_back, preferred_element_type=jnp.float32)
    d_x_one, grad_g_one, grad_b_one = ln1_pull(d_normed)
    dx_rows = (d_resid + d_x_one).astype(jnp.bfloat16)
    attn_grads = (
        lax.psum_scatter(
            grad_g_one.astype(jnp.bfloat16), "fsdp", scatter_dimension=0, tiled=True
        ).astype(jnp.float32),
        lax.psum_scatter(
            grad_b_one.astype(jnp.bfloat16), "fsdp", scatter_dimension=0, tiled=True
        ).astype(jnp.float32),
        lax.psum_scatter(
            grad_qkv.astype(jnp.bfloat16), "fsdp", scatter_dimension=0, tiled=True
        ).astype(jnp.float32),
        lax.psum_scatter(
            grad_bq.astype(jnp.bfloat16), "fsdp", scatter_dimension=0, tiled=True
        ).astype(jnp.float32),
        lax.psum_scatter(
            grad_bv.astype(jnp.bfloat16), "fsdp", scatter_dimension=0, tiled=True
        ).astype(jnp.float32),
        lax.psum_scatter(
            grad_hs.astype(jnp.bfloat16), "fsdp", scatter_dimension=0, tiled=True
        ).astype(jnp.float32),
        lax.psum_scatter(
            grad_out.astype(jnp.bfloat16), "fsdp", scatter_dimension=0, tiled=True
        ).astype(jnp.float32),
        lax.psum_scatter(
            grad_bo.astype(jnp.bfloat16), "fsdp", scatter_dimension=0, tiled=True
        ).astype(jnp.float32),
        lax.psum_scatter(
            grad_pg.astype(jnp.bfloat16), "fsdp", scatter_dimension=0, tiled=True
        ).astype(jnp.float32),
        lax.psum_scatter(
            grad_pb.astype(jnp.bfloat16), "fsdp", scatter_dimension=0, tiled=True
        ).astype(jnp.float32),
    )
    attn_grads = (
        lax.psum(attn_grads[0].astype(jnp.bfloat16), "replica").astype(jnp.float32),
        lax.psum(attn_grads[1].astype(jnp.bfloat16), "replica").astype(jnp.float32),
        lax.psum(attn_grads[2].astype(jnp.bfloat16), "replica").astype(jnp.float32),
        lax.psum(attn_grads[3].astype(jnp.bfloat16), "replica").astype(jnp.float32),
        lax.psum(attn_grads[4].astype(jnp.bfloat16), "replica").astype(jnp.float32),
        lax.psum(attn_grads[5].astype(jnp.bfloat16), "replica").astype(jnp.float32),
        lax.psum(attn_grads[6].astype(jnp.bfloat16), "replica").astype(jnp.float32),
        lax.psum(attn_grads[7].astype(jnp.bfloat16), "replica").astype(jnp.float32),
        lax.psum(attn_grads[8].astype(jnp.bfloat16), "replica").astype(jnp.float32),
        lax.psum(attn_grads[9].astype(jnp.bfloat16), "replica").astype(jnp.float32),
    )
    got_out, got_dx = (
        lax.all_to_all(
            jnp.take(out_rows, recv_order, axis=0).reshape(devices, per_pair, width),
            ("replica", "fsdp"),
            split_axis=0,
            concat_axis=0,
            tiled=True,
        ),
        lax.all_to_all(
            jnp.take(dx_rows, recv_order, axis=0).reshape(devices, per_pair, width),
            ("replica", "fsdp"),
            split_axis=0,
            concat_axis=0,
            tiled=True,
        ),
    )
    restore = jnp.argsort(send_order)
    output = jnp.take(got_out.reshape(count, width), restore, axis=0)
    grad_tokens = jnp.take(got_dx.reshape(count, width), restore, axis=0)
    return (
        output,
        grad_tokens,
        attn_grads[0],
        attn_grads[1],
        attn_grads[2],
        attn_grads[3],
        attn_grads[4],
        attn_grads[5],
        attn_grads[6],
        attn_grads[7],
        attn_grads[8],
        attn_grads[9],
        ffn_grads[0],
        ffn_grads[1],
        ffn_grads[2],
        ffn_grads[3],
        ffn_grads[4],
        ffn_grads[5],
        ffn_grads[6],
        ffn_grads[7],
    )


def solution(mesh):
    in_specs = (
        P(("replica", "fsdp"), None),
        P(("replica", "fsdp"), None),
        P(("replica", "fsdp"), None),
        P(("replica", "fsdp")),
        P(("replica", "fsdp")),
        P("fsdp"),
        P("fsdp"),
        P("fsdp", None),
        P("fsdp"),
        P("fsdp"),
        P("fsdp"),
        P("fsdp", None),
        P("fsdp"),
        P("fsdp"),
        P("fsdp"),
        P("fsdp"),
        P("fsdp"),
        P("fsdp", None),
        P("fsdp"),
        P("fsdp"),
        P("fsdp"),
        P("fsdp", None),
        P("fsdp"),
    )
    out_specs = (
        P(("replica", "fsdp"), None),
        P(("replica", "fsdp"), None),
        P("fsdp"),
        P("fsdp"),
        P("fsdp", None),
        P("fsdp"),
        P("fsdp"),
        P("fsdp"),
        P("fsdp", None),
        P("fsdp"),
        P("fsdp"),
        P("fsdp"),
        P("fsdp"),
        P("fsdp"),
        P("fsdp", None),
        P("fsdp"),
        P("fsdp"),
        P("fsdp"),
        P("fsdp", None),
        P("fsdp"),
    )
    return jax.shard_map(
        on_device, mesh=mesh, in_specs=in_specs, out_specs=out_specs, check_vma=False
    )
```

```python
import jax
import jax.numpy as jnp
from jax import lax
from jax.experimental import pallas as pl
from jax.experimental.pallas import tpu as pltpu
from jax.sharding import PartitionSpec as P

f32 = jnp.float32
bf16 = jnp.bfloat16
H = 16
HD = 64
EPS = 1e-5
NEG = -1000000000.0
NT = (((1,), (1,)), ((), ()))
NN = (((1,), (0,)), ((), ()))
TN = (((0,), (0,)), ((), ()))


def dot(a, b, dn=NN):
    return lax.dot_general(a, b, dn, preferred_element_type=f32)

def rank_row(kcol,krow):
    return jnp.sum((kcol<krow).astype(f32),axis=0,keepdims=True).astype(jnp.int32)
def rank_col(krow,kcol):
    return jnp.sum((krow<kcol).astype(f32),axis=1,keepdims=True).astype(jnp.int32)

def send_kernel(krow_ref,kcol_ref,x_ref,out_ref,rank_ref,wide_ref):
    i=pl.program_id(0); bs=out_ref.shape[0]//8
    @pl.when(i==0)
    def _(): rank_ref[...]=rank_row(kcol_ref[...],krow_ref[...])
    t=rank_ref.shape[1]
    pick=(lax.broadcasted_iota(jnp.int32,(bs,t),0)+i*bs==rank_ref[...]).astype(f32).astype(bf16)
    rows=dot(pick,x_ref[...])
    for k in range(8):
        wide_ref[pl.ds(k,bs,stride=8),:]=rows[:,128*k:128*k+128]
    out_ref[...]=wide_ref[...].astype(bf16)

def send_rows(x,keys,blocks=3):
    t,d=x.shape; bs=t//blocks
    full=lambda s:pl.BlockSpec(s,lambda i:(0,0))
    return pl.pallas_call(send_kernel,grid=(blocks,),
        in_specs=[full((1,t)),full((t,1)),full((t,d))],
        out_specs=pl.BlockSpec((bs*8,128),lambda i:(i,0)),
        out_shape=jax.ShapeDtypeStruct((t*8,128),bf16),
        scratch_shapes=[pltpu.VMEM((1,t),jnp.int32),pltpu.VMEM((bs*8,128),f32)],
        compiler_params=pltpu.CompilerParams(vmem_limit_bytes=40<<20),name="send_rows")(keys.reshape(1,t),keys.reshape(t,1),x)

def unpack_rows(got_ref,wide_ref,rows_ref,chunk=384):
    t=rows_ref.shape[0]
    for c in range(0,t,chunk):
        wide_ref[...]=got_ref[8*c:8*(c+chunk),:].astype(f32)
        for k in range(8):
            rows_ref[c:c+chunk,128*k:128*k+128]=wide_ref[pl.ds(k,chunk,stride=8),:].astype(bf16)

def recv_kernel(krow_ref,kcol_ref,got_ref,out_ref,wide_ref,rows_ref):
    i=pl.program_id(0); bs=out_ref.shape[0]
    @pl.when(i==0)
    def _(): unpack_rows(got_ref,wide_ref,rows_ref)
    t=rows_ref.shape[0]
    rank=rank_col(krow_ref[...],kcol_ref[...])
    pick=(lax.broadcasted_iota(jnp.int32,(bs,t),1)==rank).astype(f32).astype(bf16)
    out_ref[...]=dot(pick,rows_ref[...]).astype(bf16)

def recv_rows(got,keys,blocks=3):
    t=got.shape[0]//8; d=1024; bs=t//blocks
    full=lambda s:pl.BlockSpec(s,lambda i:(0,0))
    return pl.pallas_call(recv_kernel,grid=(blocks,),
        in_specs=[full((1,t)),pl.BlockSpec((bs,1),lambda i:(i,0)),full((t*8,128))],
        out_specs=pl.BlockSpec((bs,d),lambda i:(i,0)),
        out_shape=jax.ShapeDtypeStruct((t,d),bf16),
        scratch_shapes=[pltpu.VMEM((384*8,128),f32),pltpu.VMEM((t,d),bf16)],
        compiler_params=pltpu.CompilerParams(vmem_limit_bytes=40<<20),name="recv_rows")(keys.reshape(1,t),keys.reshape(t,1),got)

def norm_parts(v):
    m=jnp.mean(v,axis=-1,keepdims=True); c=v-m
    r=lax.rsqrt(jnp.mean(c*c,axis=-1,keepdims=True)+EPS)
    return c*r,r
def norm_back(e,g,vhat,r):
    eg=e*g
    return r*(eg-jnp.mean(eg,axis=-1,keepdims=True)-vhat*jnp.mean(eg*vhat,axis=-1,keepdims=True))
def colsum(v): return jnp.sum(v,axis=0,keepdims=True)

def qkv_kernel(krow_ref,kcol_ref,got_ref,vec_ref,w_ref,x_ref,a_ref,proj_ref,wide_ref,rows_ref):
    i=pl.program_id(0); bs=x_ref.shape[0]
    @pl.when(i==0)
    def _(): unpack_rows(got_ref,wide_ref,rows_ref)
    t=rows_ref.shape[0]
    rank=rank_col(krow_ref[...],kcol_ref[...])
    pick=(lax.broadcasted_iota(jnp.int32,(bs,t),1)==rank).astype(f32).astype(bf16)
    x=dot(pick,rows_ref[...])
    x_ref[...]=x.astype(bf16)
    xhat,_=norm_parts(x)
    a=(xhat*vec_ref[0:1,:]+vec_ref[1:2,:]).astype(bf16)
    a_ref[...]=a
    for j in range(3):
        w=w_ref[:,64*j:64*j+64,:].reshape(1024,1024)
        pj=dot(a,w)
        if j==0: pj=pj+vec_ref[2:3,:]
        if j==2: pj=pj+vec_ref[3:4,:]
        proj_ref[:,1024*j:1024*j+1024]=pj.astype(bf16)

def recv_qkv(got,keys,vec,pack1,blocks=3):
    t=got.shape[0]//8; d=1024; bs=t//blocks
    full=lambda s:pl.BlockSpec(s,lambda i:(0,)*len(s))
    return pl.pallas_call(qkv_kernel,grid=(blocks,),
        in_specs=[full((1,t)),pl.BlockSpec((bs,1),lambda i:(i,0)),full((t*8,128)),full(vec.shape),
                  pl.BlockSpec((16,192,1024),lambda i:(0,0,0),pipeline_mode=pl.Buffered(1))],
        out_specs=[pl.BlockSpec((bs,d),lambda i:(i,0)),pl.BlockSpec((bs,d),lambda i:(i,0)),pl.BlockSpec((bs,3*d),lambda i:(i,0))],
        out_shape=[jax.ShapeDtypeStruct((t,d),bf16),jax.ShapeDtypeStruct((t,d),bf16),jax.ShapeDtypeStruct((t,3*d),bf16)],
        scratch_shapes=[pltpu.VMEM((384*8,128),f32),pltpu.VMEM((t,d),bf16)],
        compiler_params=pltpu.CompilerParams(vmem_limit_bytes=48<<20),name="recv_qkv")(keys.reshape(1,t),keys.reshape(t,1),got,vec,pack1)

RT2=0.7071067811865476; RPI=0.3989422804014327
def mid_kernel(c_ref,o_ref,x_ref,dy_ref,vec_ref,vff_ref,w_ref,
               y_ref,a2_ref,n_ref,du_ref,dz_ref,do_ref,dres_ref,gd_ref,gf_ref,g_s,gp_s,e_s,nc=1024):
    i=pl.program_id(0)
    ff=4096
    @pl.when(i==0)
    def _():
        gd_ref[...]=jnp.zeros_like(gd_ref); gf_ref[...]=jnp.zeros_like(gf_ref)
    vec=lambda k:vec_ref[k:k+1,:]
    w_out=w_ref[:,0:64,:].reshape(1024,1024)
    w1=lambda j:w_ref[:,64+64*j:128+64*j,:].reshape(1024,1024)
    w2=lambda j:w_ref[4*j:4*j+4,320:576,:].reshape(1024,1024)
    z=dot(c_ref[...],w_out)+vec(4)
    zhat,rz=norm_parts(z)
    hres=x_ref[...].astype(f32)+zhat*vec(5)+vec(6)
    hhat,rh=norm_parts(hres)
    a2=(hhat*vec(7)+vec(8)).astype(bf16)
    a2_ref[...]=a2
    tot=0.0
    for j in range(4):
        cols=slice(1024*j,1024*j+1024)
        u=dot(a2,w1(j))+vff_ref[0:1,cols]
        phi=0.5*(1.0+lax.erf(u*RT2))
        g=u*phi
        gp_s[:,cols]=(phi+u*(RPI*jnp.exp(-0.5*u*u))).astype(gp_s.dtype)
        g_s[:,cols]=g
        tot=tot+jnp.sum(g,axis=-1,keepdims=True)
    mean=tot*(1.0/ff)
    var=0.0
    for j in range(4):
        cols=slice(1024*j,1024*j+1024)
        cen=g_s[:,cols]-mean
        var=var+jnp.sum(cen*cen,axis=-1,keepdims=True)
    rf=lax.rsqrt(var*(1.0/ff)+EPS)
    y=hres+vec(9)
    dy=dy_ref[...]
    s1=0.0; s2=0.0
    for j in range(4):
        cols=slice(1024*j,1024*j+1024)
        vhat=(g_s[:,cols]-mean)*rf
        g_s[:,cols]=vhat
        n=(vhat*vff_ref[1:2,cols]+vff_ref[2:3,cols]).astype(bf16)
        n_ref[:,cols]=n
        y=y+dot(n,w2(j))
        dn=dot(dy,w2(j),NT)
        gf_ref[0:1,cols]+=colsum(dn*vhat)
        gf_ref[1:2,cols]+=colsum(dn)
        e=dn*vff_ref[1:2,cols]
        e_s[:,cols]=e
        s1=s1+jnp.sum(e,axis=-1,keepdims=True)
        s2=s2+jnp.sum(e*vhat,axis=-1,keepdims=True)
    y_ref[...]=y.astype(bf16)
    s1=s1*(1.0/ff); s2=s2*(1.0/ff)
    da2=0.0
    for j in range(4):
        cols=slice(1024*j,1024*j+1024)
        du=(gp_s[:,cols].astype(f32)*(rf*(e_s[:,cols]-s1-g_s[:,cols]*s2))).astype(bf16)
        du_ref[:,cols]=du
        gf_ref[2:3,cols]+=colsum(du.astype(f32))
        da2=da2+dot(du,w1(j),NT)
    dyf=dy.astype(f32)
    gd_ref[0:1,:]+=colsum(dyf)
    gd_ref[1:2,:]+=colsum(da2*hhat)
    gd_ref[2:3,:]+=colsum(da2)
    dres=dyf+norm_back(da2,vec(7),hhat,rh)
    dres_ref[...]=dres
    gd_ref[3:4,:]+=colsum(dres*zhat)
    gd_ref[4:5,:]+=colsum(dres)
    dz=norm_back(dres,vec(5),zhat,rz).astype(bf16)
    dz_ref[...]=dz
    gd_ref[5:6,:]+=colsum(dz.astype(f32))
    dc=dot(dz,w_out,NT)
    gd_ref[6:7,:]+=colsum(dc*o_ref[...])
    do_ref[...]=(dc*vec(10)).astype(bf16)

def mid(c,o,x,dy,vec,vff,pack2,bm=192):
    t,d=c.shape; ff=4096
    row=lambda n:pl.BlockSpec((bm,n),lambda i:(i,0))
    full=lambda s,**k:pl.BlockSpec(s,lambda i:(0,)*len(s),**k)
    sd=jax.ShapeDtypeStruct
    return pl.pallas_call(mid_kernel,grid=(t//bm,),
        in_specs=[row(d),row(d),row(d),row(d),full(vec.shape),full(vff.shape),full(pack2.shape,pipeline_mode=pl.Buffered(1))],
        out_specs=[row(d),row(d),row(ff),row(ff),row(d),row(d),row(d),full((8,d)),full((8,ff))],
        out_shape=[sd((t,d),bf16),sd((t,d),bf16),sd((t,ff),bf16),sd((t,ff),bf16),sd((t,d),bf16),sd((t,d),bf16),sd((t,d),f32),sd((8,d),f32),sd((8,ff),f32)],
        scratch_shapes=[pltpu.VMEM((bm,ff),f32),pltpu.VMEM((bm,ff),bf16),pltpu.VMEM((bm,ff),f32)],
        compiler_params=pltpu.CompilerParams(vmem_limit_bytes=60<<20),name="mid_rows")(c,o,x,dy,vec,vff,pack2)

def dx_kernel(dq_ref,dk_ref,dv_ref,x_ref,dres_ref,vec_ref,w_ref,dx_ref,g_ref):
    i=pl.program_id(0)
    @pl.when(i==0)
    def _(): g_ref[...]=jnp.zeros_like(g_ref)
    da=0.0
    for j,r in enumerate((dq_ref,dk_ref,dv_ref)):
        da=da+dot(r[...],w_ref[:,64*j:64*j+64,:].reshape(1024,1024),NT)
    xhat,r=norm_parts(x_ref[...].astype(f32))
    g_ref[0:1,:]+=colsum(da*xhat)
    g_ref[1:2,:]+=colsum(da)
    dx_ref[...]=(dres_ref[...]+norm_back(da,vec_ref[0:1,:],xhat,r)).astype(bf16)

def dx_rows(dq,dk,dv,x,dres,vec,pack1,blocks=3):
    t,d=x.shape; bs=t//blocks
    row=pl.BlockSpec((bs,d),lambda i:(i,0))
    full=lambda s,**k:pl.BlockSpec(s,lambda i:(0,)*len(s),**k)
    return pl.pallas_call(dx_kernel,grid=(blocks,),
        in_specs=[row,row,row,row,row,full(vec.shape),full((16,192,1024),pipeline_mode=pl.Buffered(1))],
        out_specs=[row,full((8,d))],
        out_shape=[jax.ShapeDtypeStruct((t,d),bf16),jax.ShapeDtypeStruct((8,d),f32)],
        compiler_params=pltpu.CompilerParams(vmem_limit_bytes=48<<20),name="dx_rows")(dq,dk,dv,x,dres,vec,pack1)

def grad2_kernel(c_ref,dz_ref,a2_ref,du_ref,n_ref,dy_ref,out_ref):
    def put(res,at):
        for f in range(4):
            out_ref[f,at:at+64,:]=res[64*f:64*f+64,:].astype(bf16)
    put(dot(c_ref[...],dz_ref[...],TN),0)
    for j in range(4):
        put(dot(a2_ref[...],du_ref[:,1024*j:1024*j+1024],TN),64+64*j)
    res=dot(n_ref[...],dy_ref[...],TN)
    for f in range(4):
        out_ref[f,320:576,:]=res[256*f:256*f+256,:].astype(bf16)

def grad2(c,dz,a2,du,n,dy):
    t,d=c.shape
    col=lambda n:pl.BlockSpec((t,n),lambda i:(0,i))
    full=lambda s:pl.BlockSpec(s,lambda i:(0,0),pipeline_mode=pl.Buffered(1))
    return pl.pallas_call(grad2_kernel,grid=(4,),
        in_specs=[col(256),full((t,d)),col(256),full((t,4096)),col(1024),full((t,d))],
        out_specs=pl.BlockSpec((4,576,1024),lambda i:(i,0,0)),
        out_shape=jax.ShapeDtypeStruct((16,576,1024),bf16),
        compiler_params=pltpu.CompilerParams(vmem_limit_bytes=56<<20),name="grad_ffn_out")(c,dz,a2,du,n,dy)

def grad1_kernel(a_ref,dq_ref,dk_ref,dv_ref,small_ref,out_ref):
    for j,r in enumerate((dq_ref,dk_ref,dv_ref)):
        res=dot(a_ref[...],r[...],TN)
        for f in range(4):
            out_ref[f,64*j:64*j+64,:]=res[64*f:64*f+64,:].astype(bf16)
    out_ref[:,192:200,:]=small_ref[...].astype(bf16)

def grad1(a,dq,dk,dv,small):
    t,d=a.shape
    full=pl.BlockSpec((t,d),lambda i:(0,0),pipeline_mode=pl.Buffered(1))
    return pl.pallas_call(grad1_kernel,grid=(4,),
        in_specs=[pl.BlockSpec((t,256),lambda i:(0,i)),full,full,full,pl.BlockSpec((4,8,1024),lambda i:(i,0,0))],
        out_specs=pl.BlockSpec((4,200,1024),lambda i:(i,0,0)),
        out_shape=jax.ShapeDtypeStruct((16,200,1024),bf16),
        compiler_params=pltpu.CompilerParams(vmem_limit_bytes=48<<20),name="grad_qkv")(a,dq,dk,dv,small)

T=1152; D=1024
BLOCKS=[(0,256),(256,256),(512,256),(768,256),(1024,128)]


def masked_scores(sT, start_row, q0, bq):
    keys=q0+bq
    kio=lax.broadcasted_iota(jnp.int32,(128,bq),0)
    qio=lax.broadcasted_iota(jnp.int32,(1,bq),1)+q0
    parts=[]
    for k0 in range(0,keys,128):
        t=sT[k0:k0+128]
        ok=None
        if k0==0 or q0>=1024:
            ok=kio>=start_row-k0
        if k0+127>q0:
            low=kio<=qio-k0
            ok=low if ok is None else ok&low
        parts.append(t if ok is None else jnp.where(ok,t,NEG))
    return jnp.concatenate(parts,axis=0) if len(parts)>1 else parts[0]

def fwd_kernel(start_ref,hs_ref,q_ref,k_ref,v_ref,o_ref,c_ref,lse_ref):
    lane=lax.broadcasted_iota(jnp.int32,(1,128),1)
    vT=v_ref[...].T
    oT=[]
    for q0,bq in BLOCKS:
        keys=q0+bq
        k=k_ref[0:keys,:]
        qb=q_ref[q0:q0+bq,:]*jnp.asarray(HD**-0.5,bf16)
        start=start_ref[0:1,q0:q0+bq]
        halves=[]
        for h in range(2):
            qh=jnp.where((lane>=64*h)&(lane<64*h+64),qb,jnp.zeros_like(qb))
            s=masked_scores(dot(k,qh,NT),start,q0,bq)
            m=jnp.max(s,axis=0,keepdims=True)
            e=jnp.exp(s-m)
            l=jnp.sum(e,axis=0,keepdims=True)
            lse_ref[0,h:h+1,q0:q0+bq]=m+jnp.log(l)
            oh=dot(vT[64*h:64*h+64,0:keys],e.astype(bf16))
            halves.append(oh*(1.0/l))
        o=jnp.concatenate(halves,axis=0).T
        o_ref[q0:q0+bq,:]=o
        c_ref[q0:q0+bq,:]=(o*hs_ref[...]).astype(bf16)

def attn_fwd(proj,start,hs_cols):
    return pl.pallas_call(fwd_kernel,
        grid=(H//2,),
        in_specs=[pl.BlockSpec((1,T),lambda p:(0,0)),pl.BlockSpec((1,128),lambda p:(0,p)),
                  pl.BlockSpec((T,128),lambda p:(0,p)),pl.BlockSpec((T,128),lambda p:(0,8+p)),pl.BlockSpec((T,128),lambda p:(0,16+p))],
        out_specs=[pl.BlockSpec((T,128),lambda p:(0,p)),pl.BlockSpec((T,128),lambda p:(0,p)),pl.BlockSpec((1,2,T),lambda p:(p,0,0))],
        out_shape=[jax.ShapeDtypeStruct((T,D),f32),jax.ShapeDtypeStruct((T,D),bf16),jax.ShapeDtypeStruct((H//2,2,T),f32)],
        compiler_params=pltpu.CompilerParams(vmem_limit_bytes=48<<20),
        name="attn_fwd")(start,hs_cols,proj,proj,proj)

def bwd_kernel(start_ref,lse_ref,o_ref,q_ref,k_ref,v_ref,do_ref,dq_ref,dk_ref,dv_ref,bsum_ref,dk_acc,dv_acc,dqT):
    lane=lax.broadcasted_iota(jnp.int32,(1,128),1)
    scale=jnp.asarray(HD**-0.5,bf16)
    kT=(k_ref[...]*scale).T
    prodT=(o_ref[...]*do_ref[...].astype(f32)).T
    delta=[jnp.sum(prodT[64*h:64*h+64],axis=0,keepdims=True) for h in range(2)]
    dk_acc[...]=jnp.zeros_like(dk_acc)
    dv_acc[...]=jnp.zeros_like(dv_acc)
    for q0,bq in BLOCKS:
        keys=q0+bq
        k=k_ref[0:keys,:]
        v=v_ref[0:keys,:]
        qb=q_ref[q0:q0+bq,:]*scale
        dob=do_ref[q0:q0+bq,:]
        start=start_ref[0:1,q0:q0+bq]
        for h in range(2):
            half=(lane>=64*h)&(lane<64*h+64)
            qh=jnp.where(half,qb,jnp.zeros_like(qb))
            doh=jnp.where(half,dob,jnp.zeros_like(dob))
            s=masked_scores(dot(k,qh,NT),start,q0,bq)
            p=jnp.exp(s-lse_ref[0,h:h+1,q0:q0+bq])
            dp=dot(v,doh,NT)
            ds=(p*(dp-delta[h][:,q0:q0+bq])).astype(bf16)
            dv_acc[0:keys,:]+=dot(p.astype(bf16),doh)
            dk_acc[0:keys,:]+=dot(ds,qh)
            dqT[64*h:64*h+64,q0:q0+bq]=dot(kT[64*h:64*h+64,0:keys],ds)
    dq=dqT[...].T.astype(bf16)
    dk=dk_acc[...].astype(bf16)
    dv=dv_acc[...].astype(bf16)
    dq_ref[...]=dq; dk_ref[...]=dk; dv_ref[...]=dv
    bsum_ref[0:1,:]=jnp.sum(dq.astype(f32),axis=0,keepdims=True)
    bsum_ref[1:2,:]=jnp.sum(dv.astype(f32),axis=0,keepdims=True)

def attn_bwd(proj,start,lse,o,do):
    blk=lambda off:pl.BlockSpec((T,128),lambda p:(0,off+p))
    row=pl.BlockSpec((1,2,T),lambda p:(p,0,0))
    return pl.pallas_call(bwd_kernel,
        grid=(H//2,),
        in_specs=[pl.BlockSpec((1,T),lambda p:(0,0)),row,blk(0),blk(0),blk(8),blk(16),blk(0)],
        out_specs=[blk(0),blk(0),blk(0),pl.BlockSpec((2,128),lambda p:(0,p))],
        out_shape=[jax.ShapeDtypeStruct((T,D),bf16)]*3+[jax.ShapeDtypeStruct((2,D),f32)],
        scratch_shapes=[pltpu.VMEM((T,128),f32),pltpu.VMEM((T,128),f32),pltpu.VMEM((128,T),f32)],
        compiler_params=pltpu.CompilerParams(vmem_limit_bytes=48<<20),
        name="attn_bwd")(start,lse,o,proj,proj,proj,do)

BOTH = ("replica", "fsdp")


def exchange(slab, devices):
    return lax.all_to_all(slab.reshape(devices, -1, 128), BOTH, split_axis=0, concat_axis=0, tiled=True).reshape(-1, 128)


def replica_sum(part, n):
    rows, width = part.shape
    if rows % (8 * n):
        part = part.reshape(-1, 128)
    got = lax.all_to_all(part.reshape(n, -1, part.shape[1]), "replica", split_axis=0, concat_axis=0, tiled=True)
    total = jnp.sum(got.astype(f32), axis=0).astype(bf16)
    spread = jnp.broadcast_to(total[None], (n, *total.shape))
    back = lax.all_to_all(spread, "replica", split_axis=0, concat_axis=0, tiled=True)
    return back.reshape(rows, width)


def on_device(
    tokens, cotangent, lengths, deal_order, inverse, ln1_gain, ln1_bias, w_qkv, b_query, b_value, head_scale, w_out, b_out,
    post_gain, post_bias, ln2_gain, ln2_bias, w_fc1, b_fc1, ffn_gain, ffn_bias, w_fc2, b_fc2,
):
    devices = lax.axis_size(BOTH)
    replicas = lax.axis_size("replica")
    count, width = tokens.shape
    row0 = jnp.concatenate(
        [ln1_gain, ln1_bias, b_query, b_value, b_out, post_gain, post_bias, ln2_gain, ln2_bias, b_fc2, head_scale,
         jnp.zeros((383,), bf16)]
    )
    row1 = jnp.concatenate([b_fc1, ffn_gain, ffn_bias, jnp.zeros((256,), bf16)])
    small = jnp.concatenate([row0[None], row1[None], jnp.zeros((6, width), bf16)], axis=0)
    cols = lambda w, n: [w[:, width * j : width * j + width] for j in range(n)]
    pack1 = lax.all_gather(jnp.concatenate(cols(w_qkv, 3) + [small], axis=0), "fsdp", axis=0)
    recv_keys = deal_order // count * count + jnp.arange(count, dtype=jnp.int32)
    sent_x = send_rows(tokens, inverse)
    got_x = exchange(sent_x, devices)
    sent_x, w_out, w_fc1, w_fc2, cotangent = lax.optimization_barrier((sent_x, w_out, w_fc1, w_fc2, cotangent))
    pack2 = lax.all_gather(jnp.concatenate([w_out] + cols(w_fc1, 4) + [w_fc2], axis=0), "fsdp", axis=0)
    sent_dy = send_rows(cotangent, inverse)
    sent_dy, got_x = lax.optimization_barrier((sent_dy, got_x))
    got_dy = exchange(sent_dy, devices)
    vec10 = pack1[:, 192, :640].reshape(16, 10, 64).transpose(1, 0, 2).reshape(10, width).astype(f32)
    scales = jnp.repeat(pack1[:, 192, 640].astype(f32), HD)[None]
    vec = jnp.concatenate([vec10, scales, jnp.zeros((5, width), f32)], axis=0)
    vff = pack1[:, 193, :768].reshape(16, 3, 256).transpose(1, 0, 2).reshape(3, 4 * width).astype(f32)
    vff = jnp.concatenate([vff, jnp.zeros((5, 4 * width), f32)], axis=0)
    places = jnp.arange(count, dtype=jnp.int32)
    starts = jnp.zeros((count,), jnp.int32)
    seq_end = jnp.zeros((), jnp.int32)
    for i in range(lengths.shape[1]):
        seq_end = seq_end + lengths[0, i]
        starts = jnp.where(places >= seq_end, seq_end, starts)
    starts = starts.reshape(1, count)
    x_rows, a, proj = recv_qkv(got_x, recv_keys, vec, pack1)
    o, c, lse = attn_fwd(proj, starts, scales)
    got_dy, c = lax.optimization_barrier((got_dy, c))
    dy_rows = recv_rows(got_dy, recv_keys)
    y, a2, n, du, dz, do, dres, gd, gf = mid(c, o, x_rows, dy_rows, vec, vff, pack2)
    sent_y = send_rows(y, recv_keys)
    sent_y, n = lax.optimization_barrier((sent_y, n))
    got_y = exchange(sent_y, devices)
    grads2 = grad2(c, dz, a2, du, n, dy_rows)
    grads2, do = lax.optimization_barrier((grads2, do))
    part2 = lax.psum_scatter(grads2, "fsdp", scatter_dimension=0)
    dq, dk, dv, bsum = attn_bwd(proj, starts, lse, o, do)
    dx, gl = dx_rows(dq, dk, dv, x_rows, dres, vec, pack1)
    sent_dx = send_rows(dx, recv_keys)
    sent_dx, a, got_y = lax.optimization_barrier((sent_dx, a, got_y))
    got_dx = exchange(sent_dx, devices)
    ten = jnp.concatenate([gl[0:2], bsum, gd[5:6], gd[3:5], gd[1:3], gd[0:1]], axis=0)
    ten = ten.reshape(10, 16, 64).transpose(1, 0, 2).reshape(16, 640)
    heads = jnp.sum(gd[6].reshape(H, HD), axis=1, keepdims=True)
    three = jnp.concatenate([gf[2:3], gf[0:2]], axis=0).reshape(3, 16, 256).transpose(1, 0, 2).reshape(16, 768)
    line0 = jnp.concatenate([ten, heads, jnp.zeros((16, 383), f32)], axis=1)
    line1 = jnp.concatenate([three, jnp.zeros((16, 256), f32)], axis=1)
    small_grads = jnp.concatenate([line0[:, None], line1[:, None], jnp.zeros((16, 6, width), f32)], axis=1)
    grads1 = grad1(a, dq, dk, dv, small_grads)
    grads1, part2, got_dx = lax.optimization_barrier((grads1, part2, got_dx))
    part1 = lax.psum_scatter(grads1, "fsdp", scatter_dimension=0)
    sum2 = replica_sum(part2, replicas).astype(f32)
    output = recv_rows(got_y, inverse)
    grad_tokens = recv_rows(got_dx, inverse)
    sum1 = replica_sum(part1, replicas).astype(f32)
    join = lambda s, at, k: jnp.concatenate([s[at + 64 * j : at + 64 * j + 64] for j in range(k)], axis=1)
    v = [sum1[192, 64 * k : 64 * k + 64] for k in range(10)]
    w = [sum1[193, 256 * k : 256 * k + 256] for k in range(3)]
    return (
        output, grad_tokens, v[0], v[1], join(sum1, 0, 3), v[2], v[3], sum1[192, 640:641], sum2[0:64], v[4],
        v[5], v[6], v[7], v[8], join(sum2, 64, 4), w[0], w[1], w[2], sum2[320:576], v[9],
    )


def solution(mesh):
    rows, vector, matrix = P(BOTH, None), P("fsdp"), P("fsdp", None)
    in_specs = (
        rows, rows, rows, P(BOTH), P(BOTH), vector, vector, matrix, vector, vector, vector, matrix, vector, vector, vector,
        vector, vector, matrix, vector, vector, vector, matrix, vector,
    )
    out_specs = (
        rows, rows, vector, vector, matrix, vector, vector, vector, matrix, vector, vector, vector, vector, vector, matrix,
        vector, vector, vector, matrix, vector,
    )
    return jax.shard_map(on_device, mesh=mesh, in_specs=in_specs, out_specs=out_specs, check_vma=False)
```

```python
import jax
import jax.numpy as jnp
from jax import lax
from jax.experimental import pallas as pl
from jax.experimental.pallas import tpu as pltpu
from jax.sharding import PartitionSpec as P

f32 = jnp.float32
bf16 = jnp.bfloat16
H = 16
HD = 64
EPS = 1e-5
NEG = -1000000000.0
NT = (((1,), (1,)), ((), ()))
NN = (((1,), (0,)), ((), ()))
TN = (((0,), (0,)), ((), ()))


def dot(a, b, dn=NN):
    return lax.dot_general(a, b, dn, preferred_element_type=f32)


def hbm_call(kernel, **kw):
    call = pl.pallas_call(kernel, **kw)
    pin = lambda v: pltpu.with_memory_space_constraint(v, pltpu.HBM) if v.size > 1000 else v
    return lambda *args: call(*[pin(v) for v in args])


def cost(micros):
    return pl.CostEstimate(flops=0, transcendentals=0, bytes_accessed=micros * 3000000)

def rank_row(kcol,krow):
    return jnp.sum((kcol<krow).astype(f32),axis=0,keepdims=True).astype(jnp.int32)
def rank_col(krow,kcol):
    return jnp.sum((krow<kcol).astype(f32),axis=1,keepdims=True).astype(jnp.int32)

def send_kernel(krow_ref,kcol_ref,x_ref,out_ref,rank_ref,wide_ref):
    i=pl.program_id(0); bs=out_ref.shape[0]//8
    @pl.when(i==0)
    def _(): rank_ref[...]=rank_row(kcol_ref[...],krow_ref[...])
    t=rank_ref.shape[1]
    pick=(lax.broadcasted_iota(jnp.int32,(bs,t),0)+i*bs==rank_ref[...]).astype(f32).astype(bf16)
    rows=dot(pick,x_ref[...])
    for k in range(8):
        wide_ref[pl.ds(k,bs,stride=8),:]=rows[:,128*k:128*k+128]
    out_ref[...]=wide_ref[...].astype(bf16)

def send_rows(x,keys,blocks=3):
    t,d=x.shape; bs=t//blocks
    full=lambda s:pl.BlockSpec(s,lambda i:(0,0))
    return hbm_call(send_kernel,grid=(blocks,),
        in_specs=[full((1,t)),full((t,1)),full((t,d))],
        out_specs=pl.BlockSpec((bs*8,128),lambda i:(i,0)),
        out_shape=pltpu.HBM((t*8,128),bf16),
        scratch_shapes=[pltpu.VMEM((1,t),jnp.int32),pltpu.VMEM((bs*8,128),f32)],
        compiler_params=pltpu.CompilerParams(vmem_limit_bytes=40<<20),name="send_rows",cost_estimate=cost(5))(keys.reshape(1,t),keys.reshape(t,1),x)

def unpack_rows(got_ref,wide_ref,rows_ref,chunk=384):
    t=rows_ref.shape[0]
    for c in range(0,t,chunk):
        wide_ref[...]=got_ref[8*c:8*(c+chunk),:].astype(f32)
        for k in range(8):
            rows_ref[c:c+chunk,128*k:128*k+128]=wide_ref[pl.ds(k,chunk,stride=8),:].astype(bf16)

def recv_kernel(krow_ref,kcol_ref,got_ref,out_ref,wide_ref,rows_ref):
    i=pl.program_id(0); bs=out_ref.shape[0]
    @pl.when(i==0)
    def _(): unpack_rows(got_ref,wide_ref,rows_ref)
    t=rows_ref.shape[0]
    rank=rank_col(krow_ref[...],kcol_ref[...])
    pick=(lax.broadcasted_iota(jnp.int32,(bs,t),1)==rank).astype(f32).astype(bf16)
    out_ref[...]=dot(pick,rows_ref[...]).astype(bf16)

def recv_rows(got,keys,blocks=3):
    t=got.shape[0]//8; d=1024; bs=t//blocks
    full=lambda s:pl.BlockSpec(s,lambda i:(0,0))
    return hbm_call(recv_kernel,grid=(blocks,),
        in_specs=[full((1,t)),pl.BlockSpec((bs,1),lambda i:(i,0)),full((t*8,128))],
        out_specs=pl.BlockSpec((bs,d),lambda i:(i,0)),
        out_shape=pltpu.HBM((t,d),bf16),
        scratch_shapes=[pltpu.VMEM((384*8,128),f32),pltpu.VMEM((t,d),bf16)],
        compiler_params=pltpu.CompilerParams(vmem_limit_bytes=40<<20),name="recv_rows",cost_estimate=cost(6))(keys.reshape(1,t),keys.reshape(t,1),got)

def norm_parts(v):
    m=jnp.mean(v,axis=-1,keepdims=True); c=v-m
    r=lax.rsqrt(jnp.mean(c*c,axis=-1,keepdims=True)+EPS)
    return c*r,r
def norm_back(e,g,vhat,r):
    eg=e*g
    return r*(eg-jnp.mean(eg,axis=-1,keepdims=True)-vhat*jnp.mean(eg*vhat,axis=-1,keepdims=True))
def colsum(v): return jnp.sum(v,axis=0,keepdims=True)

def qkv_kernel(krow_ref,kcol_ref,got_ref,vec_ref,w_ref,x_ref,a_ref,proj_ref,wide_ref,rows_ref):
    i=pl.program_id(0); bs=x_ref.shape[0]
    @pl.when(i==0)
    def _(): unpack_rows(got_ref,wide_ref,rows_ref)
    t=rows_ref.shape[0]
    rank=rank_col(krow_ref[...],kcol_ref[...])
    pick=(lax.broadcasted_iota(jnp.int32,(bs,t),1)==rank).astype(f32).astype(bf16)
    x=dot(pick,rows_ref[...])
    x_ref[...]=x.astype(bf16)
    xhat,_=norm_parts(x)
    a=(xhat*vec_ref[0:1,:]+vec_ref[1:2,:]).astype(bf16)
    a_ref[...]=a
    for j in range(3):
        w=w_ref[:,64*j:64*j+64,:].reshape(1024,1024)
        pj=dot(a,w)
        if j==0: pj=pj+vec_ref[2:3,:]
        if j==2: pj=pj+vec_ref[3:4,:]
        proj_ref[:,1024*j:1024*j+1024]=pj.astype(bf16)

def recv_qkv(got,keys,vec,pack1,blocks=3):
    t=got.shape[0]//8; d=1024; bs=t//blocks
    full=lambda s:pl.BlockSpec(s,lambda i:(0,)*len(s))
    return hbm_call(qkv_kernel,grid=(blocks,),
        in_specs=[full((1,t)),pl.BlockSpec((bs,1),lambda i:(i,0)),full((t*8,128)),full(vec.shape),
                  pl.BlockSpec((16,192,1024),lambda i:(0,0,0),pipeline_mode=pl.Buffered(1))],
        out_specs=[pl.BlockSpec((bs,d),lambda i:(i,0)),pl.BlockSpec((bs,d),lambda i:(i,0)),pl.BlockSpec((bs,3*d),lambda i:(i,0))],
        out_shape=[pltpu.HBM((t,d),bf16),pltpu.HBM((t,d),bf16),pltpu.HBM((t,3*d),bf16)],
        scratch_shapes=[pltpu.VMEM((384*8,128),f32),pltpu.VMEM((t,d),bf16)],
        compiler_params=pltpu.CompilerParams(vmem_limit_bytes=48<<20),name="recv_qkv",cost_estimate=cost(18))(keys.reshape(1,t),keys.reshape(t,1),got,vec,pack1)

RT2=0.7071067811865476; RPI=0.3989422804014327
FF=4096
def up_kernel(c_ref,x_ref,vec_ref,w_ref,a2_ref,n_ref,vhat_ref,gp_ref,hres_ref,zhat_ref,st_ref,g_s):
    vec=lambda k:vec_ref[k:k+1,:]
    z=dot(c_ref[...],w_ref[:,0:64,:].reshape(1024,1024))+vec(4)
    zhat,rz=norm_parts(z)
    zhat_ref[...]=zhat
    hres=x_ref[...].astype(f32)+zhat*vec(5)+vec(6)
    hres_ref[...]=hres
    hhat,_=norm_parts(hres)
    a2=(hhat*vec(7)+vec(8)).astype(bf16)
    a2_ref[...]=a2
    tot=0.0
    for j in range(4):
        cols=slice(1024*j,1024*j+1024)
        u=dot(a2,w_ref[:,64+64*j:128+64*j,:].reshape(1024,1024))+vec(11+j)
        phi=0.5+0.5*lax.erf(u*RT2)
        g=u*phi
        gp_ref[:,cols]=(phi+u*(RPI*jnp.exp(-0.5*u*u))).astype(bf16)
        g_s[:,cols]=g
        tot=tot+jnp.sum(g,axis=-1,keepdims=True)
    mean=tot*(1.0/FF)
    var=0.0
    for j in range(4):
        cen=g_s[:,1024*j:1024*j+1024]-mean
        var=var+jnp.sum(cen*cen,axis=-1,keepdims=True)
    rf=lax.rsqrt(var*(1.0/FF)+EPS)
    for j in range(4):
        cols=slice(1024*j,1024*j+1024)
        vhat=(g_s[:,cols]-mean)*rf
        vhat_ref[:,cols]=vhat.astype(bf16)
        n_ref[:,cols]=(vhat*vec(15+j)+vec(19+j)).astype(bf16)
    lane=lax.broadcasted_iota(jnp.int32,(1,128),1)
    st_ref[...]=jnp.where(lane==0,rz,rf)

def row_specs(bm):
    row=lambda n:pl.BlockSpec((bm,n),lambda i:(i,0))
    full=lambda s,**k:pl.BlockSpec(s,lambda i:(0,)*len(s),**k)
    return row,full

def up_rows(c,x,vec,packa,bm=192):
    t,d=c.shape
    row,full=row_specs(bm); sd=pltpu.HBM
    return hbm_call(up_kernel,grid=(t//bm,),
        in_specs=[row(d),row(d),full(vec.shape),full(packa.shape,pipeline_mode=pl.Buffered(1))],
        out_specs=[row(d),row(FF),row(FF),row(FF),row(d),row(d),row(128)],
        out_shape=[sd((t,d),bf16),sd((t,FF),bf16),sd((t,FF),bf16),sd((t,FF),bf16),sd((t,d),f32),sd((t,d),f32),sd((t,128),f32)],
        scratch_shapes=[pltpu.VMEM((bm,FF),f32)],
        compiler_params=pltpu.CompilerParams(vmem_limit_bytes=60<<20),name="up_rows",cost_estimate=cost(45))(c,x,vec,packa)

def down_kernel(n_ref,vhat_ref,gp_ref,st_ref,dy_ref,hres_ref,vec_ref,w_ref,y_ref,du_ref,gd_ref,gf_ref,e_s):
    @pl.when(pl.program_id(0)==0)
    def _():
        gd_ref[...]=jnp.zeros_like(gd_ref); gf_ref[...]=jnp.zeros_like(gf_ref)
    vec=lambda k:vec_ref[k:k+1,:]
    rf=st_ref[:,1:2]
    dy=dy_ref[...]
    y=hres_ref[...]+vec(9)
    s1=0.0; s2=0.0
    for j in range(4):
        cols=slice(1024*j,1024*j+1024)
        w=w_ref[4*j:4*j+4].reshape(1024,1024)
        y=y+dot(n_ref[:,cols],w)
        dn=dot(dy,w,NT)
        vhat=vhat_ref[:,cols].astype(f32)
        dv=dn*vhat
        gf_ref[j:j+1,:]+=colsum(dv)
        gf_ref[4+j:5+j,:]+=colsum(dn)
        gain=vec(15+j)
        e=dn*gain
        e_s[:,cols]=e
        s1=s1+jnp.sum(e,axis=-1,keepdims=True)
        s2=s2+jnp.sum(dv*gain,axis=-1,keepdims=True)
    y_ref[...]=y.astype(bf16)
    s1=s1*(1.0/FF); s2=s2*(1.0/FF)
    for j in range(4):
        cols=slice(1024*j,1024*j+1024)
        du=(gp_ref[:,cols].astype(f32)*(rf*(e_s[:,cols]-s1-vhat_ref[:,cols].astype(f32)*s2))).astype(bf16)
        du_ref[:,cols]=du
        gf_ref[8+j:9+j,:]+=colsum(du.astype(f32))
    gd_ref[0:1,:]+=colsum(dy.astype(f32))

def down_rows(n,vhat,gp,st,dy,hres,vec,packb,bm=192):
    t,d=dy.shape
    row,full=row_specs(bm); sd=pltpu.HBM
    return hbm_call(down_kernel,grid=(t//bm,),
        in_specs=[row(FF),row(FF),row(FF),row(128),row(d),row(d),full(vec.shape),full(packb.shape,pipeline_mode=pl.Buffered(1))],
        out_specs=[row(d),row(FF),full((8,d)),full((16,d))],
        out_shape=[sd((t,d),bf16),sd((t,FF),bf16),sd((8,d),f32),sd((16,d),f32)],
        scratch_shapes=[pltpu.VMEM((bm,FF),f32)],
        compiler_params=pltpu.CompilerParams(vmem_limit_bytes=60<<20),name="down_rows",cost_estimate=cost(40))(n,vhat,gp,st,dy,hres,vec,packb)

def back_kernel(du_ref,dy_ref,hres_ref,zhat_ref,st_ref,o_ref,vec_ref,w_ref,dz_ref,do_ref,dres_ref,gd_ref):
    @pl.when(pl.program_id(0)==0)
    def _(): gd_ref[...]=jnp.zeros_like(gd_ref)
    vec=lambda k:vec_ref[k:k+1,:]
    da2=0.0
    for j in range(4):
        da2=da2+dot(du_ref[:,1024*j:1024*j+1024],w_ref[:,64+64*j:128+64*j,:].reshape(1024,1024),NT)
    hhat,rh=norm_parts(hres_ref[...])
    gd_ref[1:2,:]+=colsum(da2*hhat)
    gd_ref[2:3,:]+=colsum(da2)
    dres=dy_ref[...].astype(f32)+norm_back(da2,vec(7),hhat,rh)
    dres_ref[...]=dres
    zhat=zhat_ref[...]
    gd_ref[3:4,:]+=colsum(dres*zhat)
    gd_ref[4:5,:]+=colsum(dres)
    dz=norm_back(dres,vec(5),zhat,st_ref[:,0:1]).astype(bf16)
    dz_ref[...]=dz
    gd_ref[5:6,:]+=colsum(dz.astype(f32))
    dc=dot(dz,w_ref[:,0:64,:].reshape(1024,1024),NT)
    gd_ref[6:7,:]+=colsum(dc*o_ref[...])
    do_ref[...]=(dc*vec(10)).astype(bf16)

def back_rows(du,dy,hres,zhat,st,o,vec,packa,bm=384):
    t,d=dy.shape
    row,full=row_specs(bm); sd=pltpu.HBM
    return hbm_call(back_kernel,grid=(t//bm,),
        in_specs=[row(FF),row(d),row(d),row(d),row(128),row(d),full(vec.shape),full(packa.shape,pipeline_mode=pl.Buffered(1))],
        out_specs=[row(d),row(d),row(d),full((8,d))],
        out_shape=[sd((t,d),bf16),sd((t,d),bf16),sd((t,d),f32),sd((8,d),f32)],
        compiler_params=pltpu.CompilerParams(vmem_limit_bytes=60<<20),name="back_rows",cost_estimate=cost(25))(du,dy,hres,zhat,st,o,vec,packa)

def dx_kernel(*refs):
    *halves,x_ref,dres_ref,vec_ref,w_ref,dx_ref,g_ref=refs
    @pl.when(pl.program_id(0)==0)
    def _(): g_ref[...]=jnp.zeros_like(g_ref)
    da=0.0
    for j in range(3):
        w=w_ref[:,64*j:64*j+64,:].reshape(1024,1024)
        da=da+dot(halves[j][...],w[:,0:512],NT)+dot(halves[3+j][...],w[:,512:1024],NT)
    xhat,r=norm_parts(x_ref[...].astype(f32))
    g_ref[0:1,:]+=colsum(da*xhat)
    g_ref[1:2,:]+=colsum(da)
    dx_ref[...]=(dres_ref[...]+norm_back(da,vec_ref[0:1,:],xhat,r)).astype(bf16)

def dx_rows(halves,x,dres,vec,pack1,blocks=3):
    t,d=x.shape; bs=t//blocks
    row=lambda n:pl.BlockSpec((bs,n),lambda i:(i,0))
    full=lambda s,**k:pl.BlockSpec(s,lambda i:(0,)*len(s),**k)
    return hbm_call(dx_kernel,grid=(blocks,),
        in_specs=[row(d//2)]*6+[row(d),row(d),full(vec.shape),full((16,192,1024),pipeline_mode=pl.Buffered(1))],
        out_specs=[row(d),full((8,d))],
        out_shape=[pltpu.HBM((t,d),bf16),pltpu.HBM((8,d),f32)],
        compiler_params=pltpu.CompilerParams(vmem_limit_bytes=48<<20),name="dx_rows",cost_estimate=cost(14))(*halves,x,dres,vec,pack1)

def grad_fc2_kernel(n_ref,dy_ref,out_ref):
    res=dot(n_ref[...],dy_ref[...],TN).astype(bf16)
    for f in range(out_ref.shape[0]):
        for r in range(8):
            out_ref[f,r]=res[256*f:256*f+256,128*r:128*r+128]

def grad_fc2(n,dy,steps=4):
    t,d=dy.shape; w=FF//steps
    return hbm_call(grad_fc2_kernel,grid=(steps,),
        in_specs=[pl.BlockSpec((t,w),lambda i:(0,i)),pl.BlockSpec((t,d),lambda i:(0,0),pipeline_mode=pl.Buffered(1))],
        out_specs=pl.BlockSpec((w//256,8,256,128),lambda i:(i,0,0,0)),
        out_shape=pltpu.HBM((16,8,256,128),bf16),
        compiler_params=pltpu.CompilerParams(vmem_limit_bytes=48<<20),name="grad_fc2",cost_estimate=cost(14))(n,dy)

def grad_up_kernel(c_ref,dz_ref,a2_ref,du_ref,out_ref):
    def put(res,at):
        res=res.astype(bf16)
        for f in range(4):
            for r in range(8):
                out_ref[f,r,at:at+64,:]=res[64*f:64*f+64,128*r:128*r+128]
    put(dot(c_ref[...],dz_ref[...],TN),0)
    for j in range(4):
        put(dot(a2_ref[...],du_ref[:,1024*j:1024*j+1024],TN),64+64*j)

def grad_up(c,dz,a2,du):
    t,d=c.shape
    col=pl.BlockSpec((t,256),lambda i:(0,i))
    full=lambda s:pl.BlockSpec(s,lambda i:(0,0),pipeline_mode=pl.Buffered(1))
    return hbm_call(grad_up_kernel,grid=(4,),
        in_specs=[col,full((t,d)),col,full((t,FF))],
        out_specs=pl.BlockSpec((4,8,320,128),lambda i:(i,0,0,0)),
        out_shape=pltpu.HBM((16,8,320,128),bf16),
        compiler_params=pltpu.CompilerParams(vmem_limit_bytes=56<<20),name="grad_up",cost_estimate=cost(20))(c,dz,a2,du)

def grad_qkv_kernel(core_ref,a_ref,dq_ref,dk_ref,dv_ref,*refs):
    vecs,(keep_ref,give_ref)=refs[:-2],refs[-2:]
    i=pl.program_id(0)
    first=core_ref[0]==0
    for p,ref in enumerate((dq_ref,dk_ref,dv_ref)):
        res=dot(a_ref[...],ref[...],TN)
        for chip in range(2):
            even=res[128*chip:128*chip+64,:]; odd=res[128*chip+64:128*chip+128,:]
            mine=jnp.where(first,even,odd).astype(bf16)
            other=jnp.where(first,odd,even).astype(bf16)
            for l in range(4):
                for h in range(2):
                    q=2*(4*p+l)+h; at=32*(q%3)
                    keep_ref[q//3,chip,at:at+32,:]=mine[32*h:32*h+32,128*l:128*l+128]
                    give_ref[q//3,chip,at:at+32,:]=other[32*h:32*h+32,128*l:128*l+128]
    if vecs:
        gl_ref,b1_ref,b2_ref,gd_ref,gd0_ref,gf_ref=vecs
        for chip in range(2):
            cols=slice(128*chip,128*chip+128)
            half=jnp.where(i<2,b1_ref[:,cols],b2_ref[:,cols])
            line=lambda ref,k:ref[k:k+1,cols]
            ten=[gl_ref[0:2,cols],half,line(gd_ref,5),gd_ref[3:5,cols],gd_ref[1:3,cols],line(gd0_ref,0),line(gd_ref,6)]
            pick=lambda v,at:sum(jnp.where(i==k,gf_ref[4*v+k:4*v+k+1,at:at+128],0.0) for k in range(4))
            long=[pick(v,512*chip+128*b) for v in (2,0,1) for b in range(4)]
            rows=jnp.concatenate(ten+long+[jnp.zeros((1,128),f32)],axis=0).astype(bf16)
            for r in range(8):
                part=rows[8*r:8*r+8,:] if r<3 else jnp.zeros((8,128),bf16)
                keep_ref[r,chip,96:104,:]=part
                give_ref[r,chip,96:104,:]=part

def grad_qkv(core,a,dq,dk,dv,vecs=()):
    t,d=a.shape; w=dq.shape[1]; rows=104 if vecs else 96
    full=pl.BlockSpec((t,w),lambda i,c:(0,0),pipeline_mode=pl.Buffered(1))
    out=pl.BlockSpec((8,2,rows,128),lambda i,c:(0,i,0,0))
    lanes=lambda v:pl.BlockSpec((v.shape[0],256),lambda i,c:(0,i))
    more=[]
    if vecs:
        gl,b1,b2,gd,gd0,gf=vecs
        half=lambda lo:pl.BlockSpec((2,256),lambda i,c:(0,jnp.clip(i-lo,0,1)))
        more=[lanes(gl),half(0),half(2),lanes(gd),lanes(gd0),pl.BlockSpec(gf.shape,lambda i,c:(0,0))]
    return hbm_call(grad_qkv_kernel,
        grid_spec=pltpu.PrefetchScalarGridSpec(num_scalar_prefetch=1,grid=(4,),
            in_specs=[pl.BlockSpec((t,256),lambda i,c:(0,i)),full,full,full]+more,
            out_specs=[out,out]),
        out_shape=[pltpu.HBM((8,8,rows,128),bf16)]*2,
        compiler_params=pltpu.CompilerParams(vmem_limit_bytes=48<<20),name="grad_qkv",cost_estimate=cost(8))(core,a,dq,dk,dv,*vecs)

def totals_kernel(*refs):
    *parts,out_ref=refs
    at=0
    for p in parts:
        n=p.shape[1]
        total=jnp.sum(p[...].astype(f32),axis=0).astype(bf16)
        for r in range(8):
            out_ref[r,at:at+n,:]=total
        at+=n

def totals(parts):
    rows=sum(p.shape[1] for p in parts)
    return hbm_call(totals_kernel,out_shape=pltpu.HBM((8,rows,128),bf16),
        compiler_params=pltpu.CompilerParams(vmem_limit_bytes=40<<20),name="totals",cost_estimate=cost(4))(*parts)

def finish_kernel(core_ref,s_ref,qkv_ref,out_ref,fc1_ref,fc2_ref,ten_ref,three_ref):
    piece=lambda r,at,n:s_ref[r,at:at+n,:].astype(f32)
    for r in range(8):
        cols=slice(128*r,128*r+128)
        fc2_ref[:,cols]=piece(r,0,256)
        out_ref[:,cols]=piece(r,256,64)
        for j in range(4):
            fc1_ref[:,1024*j+128*r:1024*j+128*r+128]=piece(r,320+64*j,64)
    for half in range(2):
        for p in range(3):
            for l in range(4):
                lanes=1024*p+512*half+128*l
                for h in range(2):
                    q=2*(4*p+l)+h
                    qkv_ref[32*h:32*h+32,lanes:lanes+128]=piece(q//3,576+96*half+32*(q%3),32)
    first=core_ref[0]==0
    rows=jnp.concatenate([piece(r,768,8) for r in range(3)],axis=0)
    ten_ref[0:11,:]=jnp.where(first,rows[0:11,0:64],rows[0:11,64:128])
    ten_ref[11:16,:]=jnp.zeros((5,64),f32)
    for v in range(3):
        b=[rows[11+4*v+k:12+4*v+k,:] for k in range(4)]
        three_ref[v:v+1,0:128]=jnp.where(first,b[0],b[2])
        three_ref[v:v+1,128:256]=jnp.where(first,b[1],b[3])
    three_ref[3:8,:]=jnp.zeros((5,256),f32)

def finish(core,sums):
    sd=pltpu.HBM
    shapes=[(64,3072),(64,1024),(64,4096),(256,1024),(16,64),(8,256)]
    return hbm_call(finish_kernel,
        grid_spec=pltpu.PrefetchScalarGridSpec(num_scalar_prefetch=1,grid=(1,),
            in_specs=[pl.BlockSpec(sums.shape,lambda i,c:(0,0,0))],
            out_specs=[pl.BlockSpec(s,lambda i,c:(0,0)) for s in shapes]),
        out_shape=[sd(s,f32) for s in shapes],
        compiler_params=pltpu.CompilerParams(vmem_limit_bytes=40<<20),name="finish",cost_estimate=cost(5))(core,sums)

def pack_kernel(at_ref,*refs):
    *vecs,w_ref,out_ref=refs
    shard=at_ref[0]
    for j in range(3):
        out_ref[64*j:64*j+64,:]=w_ref[:,1024*j:1024*j+1024]
    lane=lax.broadcasted_iota(jnp.int32,(1,1024),1)
    rows=[]
    for r in vecs[:10]:
        v=r[...].astype(f32).reshape(1,-1)
        v=jnp.concatenate([v,v],axis=1)
        rows.append(jnp.where(lane//64==shard,jnp.concatenate([v]*8,axis=1),0.0))
    rows.append(jnp.where(lane//64==shard,jnp.broadcast_to(vecs[10][...].astype(f32).reshape(1,1),(1,1024)),0.0))
    for r in vecs[11:14]:
        v=jnp.concatenate([r[...].astype(f32).reshape(1,-1)]*4,axis=1)
        for j in range(4):
            rows.append(jnp.where(lane//256+4*j==shard,v,0.0))
    rows.append(jnp.zeros((1,1024),f32))
    out_ref[192:216,:]=jnp.concatenate(rows,axis=0).astype(bf16)

def pack_first(shard,vectors,w_qkv):
    full=lambda s:pl.BlockSpec(s,lambda i,c:(0,)*len(s))
    return hbm_call(pack_kernel,
        grid_spec=pltpu.PrefetchScalarGridSpec(num_scalar_prefetch=1,grid=(1,),
            in_specs=[full(v.shape) for v in vectors]+[full(w_qkv.shape)],out_specs=full((216,1024))),
        out_shape=pltpu.HBM((216,1024),bf16),name="pack_first",cost_estimate=cost(2))(shard,*vectors,w_qkv)

T=1152; D=1024
BLOCKS=[(0,256),(256,256),(512,256),(768,256),(1024,128)]


def masked_scores(sT, start_row, q0, bq):
    keys=q0+bq
    kio=lax.broadcasted_iota(jnp.int32,(128,bq),0)
    qio=lax.broadcasted_iota(jnp.int32,(1,bq),1)+q0
    parts=[]
    for k0 in range(0,keys,128):
        t=sT[k0:k0+128]
        ok=None
        if k0==0 or q0>=1024:
            ok=kio>=start_row-k0
        if k0+127>q0:
            low=kio<=qio-k0
            ok=low if ok is None else ok&low
        parts.append(t if ok is None else jnp.where(ok,t,NEG))
    return jnp.concatenate(parts,axis=0) if len(parts)>1 else parts[0]

def fwd_kernel(start_ref,hs_ref,q_ref,k_ref,v_ref,o_ref,c_ref,lse_ref):
    lane=lax.broadcasted_iota(jnp.int32,(1,128),1)
    vT=v_ref[...].T
    oT=[]
    for q0,bq in BLOCKS:
        keys=q0+bq
        k=k_ref[0:keys,:]
        qb=q_ref[q0:q0+bq,:]*jnp.asarray(HD**-0.5,bf16)
        start=start_ref[0:1,q0:q0+bq]
        halves=[]
        for h in range(2):
            qh=jnp.where((lane>=64*h)&(lane<64*h+64),qb,jnp.zeros_like(qb))
            s=masked_scores(dot(k,qh,NT),start,q0,bq)
            m=jnp.max(s,axis=0,keepdims=True)
            e=jnp.exp(s-m)
            l=jnp.sum(e,axis=0,keepdims=True)
            lse_ref[0,h:h+1,q0:q0+bq]=m+jnp.log(l)
            oh=dot(vT[64*h:64*h+64,0:keys],e.astype(bf16))
            halves.append(oh*(1.0/l))
        o=jnp.concatenate(halves,axis=0).T
        o_ref[q0:q0+bq,:]=o
        c_ref[q0:q0+bq,:]=(o*hs_ref[10:11,:]).astype(bf16)

def attn_fwd(proj,start,hs_cols):
    return hbm_call(fwd_kernel,
        grid=(H//2,),
        in_specs=[pl.BlockSpec((1,T),lambda p:(0,0)),pl.BlockSpec((24,128),lambda p:(0,p)),
                  pl.BlockSpec((T,128),lambda p:(0,p)),pl.BlockSpec((T,128),lambda p:(0,8+p)),pl.BlockSpec((T,128),lambda p:(0,16+p))],
        out_specs=[pl.BlockSpec((T,128),lambda p:(0,p)),pl.BlockSpec((T,128),lambda p:(0,p)),pl.BlockSpec((1,2,T),lambda p:(p,0,0))],
        out_shape=[pltpu.HBM((T,D),f32),pltpu.HBM((T,D),bf16),pltpu.HBM((H//2,2,T),f32)],
        compiler_params=pltpu.CompilerParams(vmem_limit_bytes=48<<20),
        name="attn_fwd",cost_estimate=cost(40))(start,hs_cols,proj,proj,proj)

def bwd_kernel(start_ref,lse_ref,o_ref,q_ref,k_ref,v_ref,do_ref,dq_ref,dk_ref,dv_ref,bsum_ref,dk_acc,dv_acc,dqT):
    lane=lax.broadcasted_iota(jnp.int32,(1,128),1)
    scale=jnp.asarray(HD**-0.5,bf16)
    kT=(k_ref[...]*scale).T
    prodT=(o_ref[...]*do_ref[...].astype(f32)).T
    delta=[jnp.sum(prodT[64*h:64*h+64],axis=0,keepdims=True) for h in range(2)]
    dk_acc[...]=jnp.zeros_like(dk_acc)
    dv_acc[...]=jnp.zeros_like(dv_acc)
    for q0,bq in BLOCKS:
        keys=q0+bq
        k=k_ref[0:keys,:]
        v=v_ref[0:keys,:]
        qb=q_ref[q0:q0+bq,:]*scale
        dob=do_ref[q0:q0+bq,:]
        start=start_ref[0:1,q0:q0+bq]
        for h in range(2):
            half=(lane>=64*h)&(lane<64*h+64)
            qh=jnp.where(half,qb,jnp.zeros_like(qb))
            doh=jnp.where(half,dob,jnp.zeros_like(dob))
            s=masked_scores(dot(k,qh,NT),start,q0,bq)
            p=jnp.exp(s-lse_ref[0,h:h+1,q0:q0+bq])
            dp=dot(v,doh,NT)
            ds=(p*(dp-delta[h][:,q0:q0+bq])).astype(bf16)
            dv_acc[0:keys,:]+=dot(p.astype(bf16),doh)
            dk_acc[0:keys,:]+=dot(ds,qh)
            dqT[64*h:64*h+64,q0:q0+bq]=dot(kT[64*h:64*h+64,0:keys],ds)
    dq=dqT[...].T.astype(bf16)
    dk=dk_acc[...].astype(bf16)
    dv=dv_acc[...].astype(bf16)
    dq_ref[...]=dq; dk_ref[...]=dk; dv_ref[...]=dv
    bsum_ref[0:1,:]=jnp.sum(dq.astype(f32),axis=0,keepdims=True)
    bsum_ref[1:2,:]=jnp.sum(dv.astype(f32),axis=0,keepdims=True)

def attn_bwd(proj,start,lse,o,do,half):
    pairs=H//4; at=half*pairs
    blk=lambda off:pl.BlockSpec((T,128),lambda p:(0,off+at+p))
    out=pl.BlockSpec((T,128),lambda p:(0,p))
    return hbm_call(bwd_kernel,
        grid=(pairs,),
        in_specs=[pl.BlockSpec((1,T),lambda p:(0,0)),pl.BlockSpec((1,2,T),lambda p:(at+p,0,0)),blk(0),blk(0),blk(8),blk(16),blk(0)],
        out_specs=[out,out,out,pl.BlockSpec((2,128),lambda p:(0,p))],
        out_shape=[pltpu.HBM((T,D//2),bf16)]*3+[pltpu.HBM((2,D//2),f32)],
        scratch_shapes=[pltpu.VMEM((T,128),f32),pltpu.VMEM((T,128),f32),pltpu.VMEM((128,T),f32)],
        compiler_params=pltpu.CompilerParams(vmem_limit_bytes=48<<20),
        name="attn_bwd",cost_estimate=cost(20))(start,lse,o,proj,proj,proj,do)

EVERY = ("replica", "chip", "core")
SHARD = ("chip", "core")
PEERS = ("replica", "chip")


def exchange(slab, devices):
    return lax.all_to_all(slab.reshape(devices, -1, 128), EVERY, split_axis=0, concat_axis=0, tiled=True).reshape(-1, 128)


def replica_parts(part):
    return lax.all_to_all(part, "replica", split_axis=0, concat_axis=0, tiled=True)


def core_sum(keep, give):
    taken = lax.ppermute(give, "core", [(0, 1), (1, 0)])
    both = keep.astype(f32) + taken.astype(f32)
    return both.astype(bf16).reshape(64, *keep.shape[2:])


def peer_parts(both):
    return lax.all_to_all(both, PEERS, split_axis=0, concat_axis=0, tiled=True)


def on_device(
    tokens, cotangent, lengths, deal_order, inverse, ln1_gain, ln1_bias, w_qkv, b_query, b_value, head_scale, w_out, b_out,
    post_gain, post_bias, ln2_gain, ln2_bias, w_fc1, b_fc1, ffn_gain, ffn_bias, w_fc2, b_fc2,
):
    devices = lax.axis_size(EVERY)
    replicas = lax.axis_size("replica")
    count, width = tokens.shape
    core = lax.axis_index("core").astype(jnp.int32).reshape(1)
    shard = lax.axis_index(SHARD).astype(jnp.int32).reshape(1)
    vectors = [ln1_gain, ln1_bias, b_query, b_value, b_out, post_gain, post_bias, ln2_gain, ln2_bias, b_fc2, head_scale,
               b_fc1, ffn_gain, ffn_bias]
    first = pack_first(shard, vectors, w_qkv)
    pack1 = lax.all_gather(first, SHARD, axis=0)
    recv_keys = deal_order // count * count + jnp.arange(count, dtype=jnp.int32)
    first, tokens = lax.optimization_barrier((first, tokens))
    sent_x = send_rows(tokens, inverse)
    got_x = exchange(sent_x, devices)
    sent_x, w_out, w_fc1, cotangent = lax.optimization_barrier((sent_x, w_out, w_fc1, cotangent))
    packa = lax.all_gather(jnp.concatenate([w_out] + [w_fc1[:, width * j : width * j + width] for j in range(4)], axis=0), SHARD, axis=0)
    packb = lax.all_gather(w_fc2, SHARD, axis=0)
    sent_dy = send_rows(cotangent, inverse)
    sent_dy, got_x, pack1 = lax.optimization_barrier((sent_dy, got_x, pack1))
    got_dy = exchange(sent_dy, devices)
    vec = jnp.sum(pack1[:, 192:216].astype(f32), axis=0)
    places = jnp.arange(count, dtype=jnp.int32)
    starts = jnp.zeros((count,), jnp.int32)
    seq_end = jnp.zeros((), jnp.int32)
    for i in range(lengths.shape[1]):
        seq_end = seq_end + lengths[0, i]
        starts = jnp.where(places >= seq_end, seq_end, starts)
    starts = starts.reshape(1, count)
    x_rows, a, proj = recv_qkv(got_x, recv_keys, vec, pack1)
    o, c, lse = attn_fwd(proj, starts, vec)
    got_dy, c = lax.optimization_barrier((got_dy, c))
    dy_rows = recv_rows(got_dy, recv_keys)
    a2, n, vhat, gp, hres, zhat, stats = up_rows(c, x_rows, vec, packa)
    grads_fc2 = grad_fc2(n, dy_rows)
    grads_fc2, gp = lax.optimization_barrier((grads_fc2, gp))
    part_fc2 = lax.psum_scatter(grads_fc2, SHARD, scatter_dimension=0)
    y, du, gd0, gf = down_rows(n, vhat, gp, stats, dy_rows, hres, vec, packb)
    sent_y = send_rows(y, recv_keys)
    sent_y, du = lax.optimization_barrier((sent_y, du))
    got_y = exchange(sent_y, devices)
    dz, do, dres, gd = back_rows(du, dy_rows, hres, zhat, stats, o, vec, packa)
    grads_up = grad_up(c, dz, a2, du)
    grads_up, do, got_y = lax.optimization_barrier((grads_up, do, got_y))
    grads_up, part_fc2 = lax.optimization_barrier((grads_up, part_fc2))
    part_up = lax.psum_scatter(grads_up, SHARD, scatter_dimension=0)
    parts_fc2 = replica_parts(part_fc2)
    halves1 = attn_bwd(proj, starts, lse, o, do, 0)
    dq1, parts_fc2 = lax.optimization_barrier((halves1[0], parts_fc2))
    both1 = core_sum(*grad_qkv(core, a, dq1, *halves1[1:3]))
    parts1 = peer_parts(both1)
    both1, do = lax.optimization_barrier((both1, do))
    halves2 = attn_bwd(proj, starts, lse, o, do, 1)
    dq2, parts1 = lax.optimization_barrier((halves2[0], parts1))
    dx, gl = dx_rows([dq1, *halves1[1:3], dq2, *halves2[1:3]], x_rows, dres, vec, pack1)
    sent_dx = send_rows(dx, recv_keys)
    sent_dx, gl = lax.optimization_barrier((sent_dx, gl))
    got_dx = exchange(sent_dx, devices)
    both2 = core_sum(*grad_qkv(core, a, dq2, *halves2[1:3], (gl, halves1[3], halves2[3], gd, gd0, gf)))
    both2, got_y = lax.optimization_barrier((both2, got_y))
    output = recv_rows(got_y, inverse)
    both2, got_dx, output = lax.optimization_barrier((both2, got_dx, output))
    parts_up = replica_parts(part_up)
    both2, parts_up = lax.optimization_barrier((both2, parts_up))
    parts2 = peer_parts(both2)
    spread = totals([parts_fc2, parts_up, parts1, parts2])
    sums = lax.all_to_all(spread, "replica", split_axis=0, concat_axis=0, tiled=True)
    grad_tokens = recv_rows(got_dx, inverse)
    g_qkv, g_out, g_fc1, g_fc2, ten, three = finish(core, sums)
    v = [ten[k] for k in range(10)]
    return (
        output, grad_tokens, v[0], v[1], g_qkv, v[2], v[3], jnp.sum(ten[10]).reshape(1), g_out, v[4], v[5], v[6], v[7], v[8], g_fc1,
        three[0], three[1], three[2], g_fc2, v[9],
    )


def solution(mesh):
    replicas, shards = mesh.devices.shape
    mesh = jax.sharding.Mesh(mesh.devices.reshape(replicas, shards // 2, 2), EVERY)
    rows, vector, matrix = P(EVERY, None), P(SHARD), P(SHARD, None)
    in_specs = (
        rows, rows, rows, P(EVERY), P(EVERY), vector, vector, matrix, vector, vector, vector, matrix, vector, vector, vector,
        vector, vector, matrix, vector, vector, vector, matrix, vector,
    )
    out_specs = (
        rows, rows, vector, vector, matrix, vector, vector, vector, matrix, vector, vector, vector, vector, vector, matrix,
        vector, vector, vector, matrix, vector,
    )
    return jax.shard_map(on_device, mesh=mesh, in_specs=in_specs, out_specs=out_specs, check_vma=False)
```

```python
import jax
import jax.numpy as jnp
from jax import lax
from jax.experimental import pallas as pl
from jax.experimental.pallas import tpu as pltpu
from jax.sharding import PartitionSpec as P

f32 = jnp.float32
bf16 = jnp.bfloat16
H = 16
HD = 64
EPS = 1e-5
NEG = -1000000000.0
NT = (((1,), (1,)), ((), ()))
NN = (((1,), (0,)), ((), ()))
TN = (((0,), (0,)), ((), ()))


def dot(a, b, dn=NN):
    return lax.dot_general(a, b, dn, preferred_element_type=f32)


def hbm_call(kernel, **kw):
    call = pl.pallas_call(kernel, **kw)
    pin = lambda v: pltpu.with_memory_space_constraint(v, pltpu.HBM) if v.size > 1000 else v
    return lambda *args: call(*[pin(v) for v in args])


def cost(micros):
    return pl.CostEstimate(flops=0, transcendentals=0, bytes_accessed=micros * 3000000)

def rank_row(kcol,krow):
    return jnp.sum((kcol<krow).astype(f32),axis=0,keepdims=True).astype(jnp.int32)
def rank_col(krow,kcol):
    return jnp.sum((krow<kcol).astype(f32),axis=1,keepdims=True).astype(jnp.int32)

def send_kernel(krow_ref,kcol_ref,x_ref,out_ref,rank_ref,wide_ref):
    i=pl.program_id(0); bs=out_ref.shape[0]//8
    @pl.when(i==0)
    def _(): rank_ref[...]=rank_row(kcol_ref[...],krow_ref[...])
    t=rank_ref.shape[1]
    pick=(lax.broadcasted_iota(jnp.int32,(bs,t),0)+i*bs==rank_ref[...]).astype(f32).astype(bf16)
    rows=dot(pick,x_ref[...])
    for k in range(8):
        wide_ref[pl.ds(k,bs,stride=8),:]=rows[:,128*k:128*k+128]
    out_ref[...]=wide_ref[...].astype(bf16)

def send_rows(x,keys,blocks=3):
    t,d=x.shape; bs=t//blocks
    full=lambda s:pl.BlockSpec(s,lambda i:(0,0))
    return hbm_call(send_kernel,grid=(blocks,),
        in_specs=[full((1,t)),full((t,1)),full((t,d))],
        out_specs=pl.BlockSpec((bs*8,128),lambda i:(i,0)),
        out_shape=pltpu.HBM((t*8,128),bf16),
        scratch_shapes=[pltpu.VMEM((1,t),jnp.int32),pltpu.VMEM((bs*8,128),f32)],
        compiler_params=pltpu.CompilerParams(vmem_limit_bytes=40<<20),name="send_rows",cost_estimate=cost(5))(keys.reshape(1,t),keys.reshape(t,1),x)

def unpack_rows(got_ref,wide_ref,rows_ref,chunk=384):
    t=rows_ref.shape[0]
    for c in range(0,t,chunk):
        wide_ref[...]=got_ref[8*c:8*(c+chunk),:].astype(f32)
        for k in range(8):
            rows_ref[c:c+chunk,128*k:128*k+128]=wide_ref[pl.ds(k,chunk,stride=8),:].astype(bf16)

def recv_kernel(krow_ref,kcol_ref,got_ref,out_ref,wide_ref,rows_ref):
    i=pl.program_id(0); bs=out_ref.shape[0]
    @pl.when(i==0)
    def _(): unpack_rows(got_ref,wide_ref,rows_ref)
    t=rows_ref.shape[0]
    rank=rank_col(krow_ref[...],kcol_ref[...])
    pick=(lax.broadcasted_iota(jnp.int32,(bs,t),1)==rank).astype(f32).astype(bf16)
    out_ref[...]=dot(pick,rows_ref[...]).astype(bf16)

def recv_rows(got,keys,blocks=3):
    t=got.shape[0]//8; d=1024; bs=t//blocks
    full=lambda s:pl.BlockSpec(s,lambda i:(0,0))
    return hbm_call(recv_kernel,grid=(blocks,),
        in_specs=[full((1,t)),pl.BlockSpec((bs,1),lambda i:(i,0)),full((t*8,128))],
        out_specs=pl.BlockSpec((bs,d),lambda i:(i,0)),
        out_shape=pltpu.HBM((t,d),bf16),
        scratch_shapes=[pltpu.VMEM((384*8,128),f32),pltpu.VMEM((t,d),bf16)],
        compiler_params=pltpu.CompilerParams(vmem_limit_bytes=40<<20),name="recv_rows",cost_estimate=cost(6))(keys.reshape(1,t),keys.reshape(t,1),got)

def send_more_kernel(krow_ref,kcol_ref,x_ref,more_ref,out_ref,rank_ref,wide_ref):
    i=pl.program_id(0); slabs=out_ref.shape[0]; bs=slabs*9
    @pl.when(i==0)
    def _(): rank_ref[...]=rank_row(kcol_ref[...],krow_ref[...])
    t=rank_ref.shape[1]
    pick=(lax.broadcasted_iota(jnp.int32,(bs,t),0)+i*bs==rank_ref[...]).astype(f32).astype(bf16)
    rows=dot(pick,x_ref[...])
    for k in range(8):
        wide_ref[pl.ds(k,bs,stride=8),:]=rows[:,128*k:128*k+128]
    out_ref[:,0:72,:]=wide_ref[...].astype(bf16).reshape(slabs,72,128)
    more=more_ref[...].astype(bf16)
    for d in range(slabs):
        chip=d%16//2
        out_ref[d,72:80,:]=more[:,128*chip:128*chip+128]

def send_more(x,keys,more,blocks=4):
    t,d=x.shape; bs=t//blocks
    full=lambda s:pl.BlockSpec(s,lambda i:(0,0))
    return hbm_call(send_more_kernel,grid=(blocks,),
        in_specs=[full((1,t)),full((t,1)),full((t,d)),full((8,d))],
        out_specs=pl.BlockSpec((bs//9,80,128),lambda i:(i,0,0)),
        out_shape=pltpu.HBM((t//9,80,128),bf16),
        scratch_shapes=[pltpu.VMEM((1,t),jnp.int32),pltpu.VMEM((bs*8,128),f32)],
        compiler_params=pltpu.CompilerParams(vmem_limit_bytes=40<<20),name="send_more",cost_estimate=cost(5))(keys.reshape(1,t),keys.reshape(t,1),x,more)

def recv_more_kernel(krow_ref,kcol_ref,got_ref,out_ref,more_ref,wide_ref,rows_ref):
    i=pl.program_id(0); bs=out_ref.shape[0]; t=rows_ref.shape[0]
    @pl.when(i==0)
    def _():
        for c in range(0,t,288):
            wide_ref[...]=got_ref[c//9:c//9+32,0:72,:].reshape(288*8,128).astype(f32)
            for k in range(8):
                rows_ref[c:c+288,128*k:128*k+128]=wide_ref[pl.ds(k,288,stride=8),:].astype(bf16)
        more_ref[...]=jnp.sum(got_ref[:,72:80,:].astype(f32),axis=0)
    rank=rank_col(krow_ref[...],kcol_ref[...])
    pick=(lax.broadcasted_iota(jnp.int32,(bs,t),1)==rank).astype(f32).astype(bf16)
    out_ref[...]=dot(pick,rows_ref[...]).astype(bf16)

def recv_more(got,keys,blocks=3):
    t=got.shape[0]*9; d=1024; bs=t//blocks
    full=lambda s:pl.BlockSpec(s,lambda i:(0,)*len(s))
    return hbm_call(recv_more_kernel,grid=(blocks,),
        in_specs=[full((1,t)),pl.BlockSpec((bs,1),lambda i:(i,0)),full(got.shape)],
        out_specs=[pl.BlockSpec((bs,d),lambda i:(i,0)),full((8,128))],
        out_shape=[pltpu.HBM((t,d),bf16),pltpu.HBM((8,128),f32)],
        scratch_shapes=[pltpu.VMEM((288*8,128),f32),pltpu.VMEM((t,d),bf16)],
        compiler_params=pltpu.CompilerParams(vmem_limit_bytes=40<<20),name="recv_more",cost_estimate=cost(6))(keys.reshape(1,t),keys.reshape(t,1),got)

def norm_parts(v):
    m=jnp.mean(v,axis=-1,keepdims=True); c=v-m
    r=lax.rsqrt(jnp.mean(c*c,axis=-1,keepdims=True)+EPS)
    return c*r,r
def norm_back(e,g,vhat,r):
    eg=e*g
    return r*(eg-jnp.mean(eg,axis=-1,keepdims=True)-vhat*jnp.mean(eg*vhat,axis=-1,keepdims=True))
def colsum(v): return jnp.sum(v,axis=0,keepdims=True)

def qkv_kernel(krow_ref,kcol_ref,got_ref,vec_ref,w_ref,x_ref,a_ref,proj_ref,wide_ref,rows_ref):
    i=pl.program_id(0); bs=x_ref.shape[0]
    @pl.when(i==0)
    def _(): unpack_rows(got_ref,wide_ref,rows_ref)
    t=rows_ref.shape[0]
    rank=rank_col(krow_ref[...],kcol_ref[...])
    pick=(lax.broadcasted_iota(jnp.int32,(bs,t),1)==rank).astype(f32).astype(bf16)
    x=dot(pick,rows_ref[...])
    x_ref[...]=x.astype(bf16)
    xhat,_=norm_parts(x)
    a=(xhat*vec_ref[0:1,:]+vec_ref[1:2,:]).astype(bf16)
    a_ref[...]=a
    for j in range(3):
        w=w_ref[:,64*j:64*j+64,:].reshape(1024,1024)
        pj=dot(a,w)
        if j==0: pj=pj+vec_ref[2:3,:]
        if j==2: pj=pj+vec_ref[3:4,:]
        proj_ref[:,1024*j:1024*j+1024]=pj.astype(bf16)

def recv_qkv(got,keys,vec,pack1,blocks=3):
    t=got.shape[0]//8; d=1024; bs=t//blocks
    full=lambda s:pl.BlockSpec(s,lambda i:(0,)*len(s))
    return hbm_call(qkv_kernel,grid=(blocks,),
        in_specs=[full((1,t)),pl.BlockSpec((bs,1),lambda i:(i,0)),full((t*8,128)),full(vec.shape),
                  pl.BlockSpec((16,192,1024),lambda i:(0,0,0),pipeline_mode=pl.Buffered(1))],
        out_specs=[pl.BlockSpec((bs,d),lambda i:(i,0)),pl.BlockSpec((bs,d),lambda i:(i,0)),pl.BlockSpec((bs,3*d),lambda i:(i,0))],
        out_shape=[pltpu.HBM((t,d),bf16),pltpu.HBM((t,d),bf16),pltpu.HBM((t,3*d),bf16)],
        scratch_shapes=[pltpu.VMEM((384*8,128),f32),pltpu.VMEM((t,d),bf16)],
        compiler_params=pltpu.CompilerParams(vmem_limit_bytes=48<<20),name="recv_qkv",cost_estimate=cost(18))(keys.reshape(1,t),keys.reshape(t,1),got,vec,pack1)

RT2=0.7071067811865476; RPI=0.3989422804014327
FF=4096
def up_kernel(c_ref,x_ref,vec_ref,w_ref,a2_ref,n_ref,vhat_ref,gp_ref,hres_ref,zhat_ref,st_ref,g_s):
    vec=lambda k:vec_ref[k:k+1,:]
    z=dot(c_ref[...],w_ref[:,0:64,:].reshape(1024,1024))+vec(4)
    zhat,rz=norm_parts(z)
    zhat_ref[...]=zhat
    hres=x_ref[...].astype(f32)+zhat*vec(5)+vec(6)
    hres_ref[...]=hres
    hhat,_=norm_parts(hres)
    a2=(hhat*vec(7)+vec(8)).astype(bf16)
    a2_ref[...]=a2
    tot=0.0
    for j in range(4):
        cols=slice(1024*j,1024*j+1024)
        u=dot(a2,w_ref[:,64+64*j:128+64*j,:].reshape(1024,1024))+vec(11+j)
        phi=0.5+0.5*lax.erf(u*RT2)
        g=u*phi
        gp_ref[:,cols]=(phi+u*(RPI*jnp.exp(-0.5*u*u))).astype(bf16)
        g_s[:,cols]=g
        tot=tot+jnp.sum(g,axis=-1,keepdims=True)
    mean=tot*(1.0/FF)
    var=0.0
    for j in range(4):
        cen=g_s[:,1024*j:1024*j+1024]-mean
        var=var+jnp.sum(cen*cen,axis=-1,keepdims=True)
    rf=lax.rsqrt(var*(1.0/FF)+EPS)
    for j in range(4):
        cols=slice(1024*j,1024*j+1024)
        vhat=(g_s[:,cols]-mean)*rf
        vhat_ref[:,cols]=vhat.astype(bf16)
        n_ref[:,cols]=(vhat*vec(15+j)+vec(19+j)).astype(bf16)
    lane=lax.broadcasted_iota(jnp.int32,(1,128),1)
    st_ref[...]=jnp.where(lane==0,rz,rf)

def row_specs(bm):
    row=lambda n:pl.BlockSpec((bm,n),lambda i:(i,0))
    full=lambda s,**k:pl.BlockSpec(s,lambda i:(0,)*len(s),**k)
    return row,full

def up_rows(c,x,vec,packa,bm=384):
    t,d=c.shape
    row,full=row_specs(bm); sd=pltpu.HBM
    return hbm_call(up_kernel,grid=(t//bm,),
        in_specs=[row(d),row(d),full(vec.shape),full(packa.shape,pipeline_mode=pl.Buffered(1))],
        out_specs=[row(d),row(FF),row(FF),row(FF),row(d),row(d),row(128)],
        out_shape=[sd((t,d),bf16),sd((t,FF),bf16),sd((t,FF),bf16),sd((t,FF),bf16),sd((t,d),f32),sd((t,d),f32),sd((t,128),f32)],
        scratch_shapes=[pltpu.VMEM((bm,FF),f32)],
        compiler_params=pltpu.CompilerParams(vmem_limit_bytes=60<<20),name="up_rows",cost_estimate=cost(45))(c,x,vec,packa)

def down_kernel(n_ref,vhat_ref,gp_ref,st_ref,dy_ref,hres_ref,vec_ref,w_ref,y_ref,du_ref,gd_ref,gf_ref,e_s):
    @pl.when(pl.program_id(0)==0)
    def _():
        gd_ref[...]=jnp.zeros_like(gd_ref); gf_ref[...]=jnp.zeros_like(gf_ref)
    vec=lambda k:vec_ref[k:k+1,:]
    rf=st_ref[:,1:2]
    dy=dy_ref[...]
    w=lambda j:w_ref[4*j:4*j+4].reshape(1024,1024)
    s1=0.0; s2=0.0
    dn=dot(dy,w(0),NT)
    for j in range(4):
        cols=slice(1024*j,1024*j+1024)
        ahead=dot(dy,w(j+1),NT) if j<3 else None
        dv=dn*vhat_ref[:,cols].astype(f32)
        gf_ref[j:j+1,:]+=colsum(dv)
        gf_ref[4+j:5+j,:]+=colsum(dn)
        gain=vec(15+j)
        e=dn*gain
        e_s[:,cols]=e
        s1=s1+jnp.sum(e,axis=-1,keepdims=True)
        s2=s2+jnp.sum(dv*gain,axis=-1,keepdims=True)
        dn=ahead
    s1=rf*s1*(1.0/FF); s2=rf*s2*(1.0/FF)
    y=hres_ref[...]+vec(9)
    for j in range(4):
        cols=slice(1024*j,1024*j+1024)
        y=y+dot(n_ref[:,cols],w(j))
        du=gp_ref[:,cols].astype(f32)*(rf*e_s[:,cols]-s1-vhat_ref[:,cols].astype(f32)*s2)
        du_ref[:,cols]=du.astype(bf16)
        gf_ref[8+j:9+j,:]+=colsum(du)
    y_ref[...]=y.astype(bf16)
    gd_ref[0:1,:]+=colsum(dy.astype(f32))

def down_rows(n,vhat,gp,st,dy,hres,vec,packb,bm=288):
    t,d=dy.shape
    row,full=row_specs(bm); sd=pltpu.HBM
    return hbm_call(down_kernel,grid=(t//bm,),
        in_specs=[row(FF),row(FF),row(FF),row(128),row(d),row(d),full(vec.shape),full(packb.shape,pipeline_mode=pl.Buffered(1))],
        out_specs=[row(d),row(FF),full((8,d)),full((16,d))],
        out_shape=[sd((t,d),bf16),sd((t,FF),bf16),sd((8,d),f32),sd((16,d),f32)],
        scratch_shapes=[pltpu.VMEM((bm,FF),f32)],
        compiler_params=pltpu.CompilerParams(vmem_limit_bytes=60<<20),name="down_rows",cost_estimate=cost(40))(n,vhat,gp,st,dy,hres,vec,packb)

def back_kernel(du_ref,dy_ref,hres_ref,zhat_ref,st_ref,o_ref,vec_ref,w_ref,dz_ref,do_ref,dres_ref,gd_ref):
    @pl.when(pl.program_id(0)==0)
    def _(): gd_ref[...]=jnp.zeros_like(gd_ref)
    vec=lambda k:vec_ref[k:k+1,:]
    da2=0.0
    for j in range(4):
        da2=da2+dot(du_ref[:,1024*j:1024*j+1024],w_ref[:,64+64*j:128+64*j,:].reshape(1024,1024),NT)
    hhat,rh=norm_parts(hres_ref[...])
    gd_ref[1:2,:]+=colsum(da2*hhat)
    gd_ref[2:3,:]+=colsum(da2)
    dres=dy_ref[...].astype(f32)+norm_back(da2,vec(7),hhat,rh)
    dres_ref[...]=dres
    zhat=zhat_ref[...]
    gd_ref[3:4,:]+=colsum(dres*zhat)
    gd_ref[4:5,:]+=colsum(dres)
    dz=norm_back(dres,vec(5),zhat,st_ref[:,0:1]).astype(bf16)
    dz_ref[...]=dz
    gd_ref[5:6,:]+=colsum(dz.astype(f32))
    dc=dot(dz,w_ref[:,0:64,:].reshape(1024,1024),NT)
    gd_ref[6:7,:]+=colsum(dc*o_ref[...])
    do_ref[...]=(dc*vec(10)).astype(bf16)

def back_rows(du,dy,hres,zhat,st,o,vec,packa,bm=288):
    t,d=dy.shape
    row,full=row_specs(bm); sd=pltpu.HBM
    return hbm_call(back_kernel,grid=(t//bm,),
        in_specs=[row(FF),row(d),row(d),row(d),row(128),row(d),full(vec.shape),full(packa.shape,pipeline_mode=pl.Buffered(1))],
        out_specs=[row(d),row(d),row(d),full((8,d))],
        out_shape=[sd((t,d),bf16),sd((t,d),bf16),sd((t,d),f32),sd((8,d),f32)],
        compiler_params=pltpu.CompilerParams(vmem_limit_bytes=60<<20),name="back_rows",cost_estimate=cost(25))(du,dy,hres,zhat,st,o,vec,packa)

def dx_kernel(*refs):
    *halves,x_ref,dres_ref,vec_ref,w_ref,dx_ref,g_ref=refs
    @pl.when(pl.program_id(0)==0)
    def _(): g_ref[...]=jnp.zeros_like(g_ref)
    da=0.0
    for j in range(3):
        w=w_ref[:,64*j:64*j+64,:].reshape(1024,1024)
        da=da+dot(halves[j][...],w[:,0:512],NT)+dot(halves[3+j][...],w[:,512:1024],NT)
    xhat,r=norm_parts(x_ref[...].astype(f32))
    g_ref[0:1,:]+=colsum(da*xhat)
    g_ref[1:2,:]+=colsum(da)
    dx_ref[...]=(dres_ref[...]+norm_back(da,vec_ref[0:1,:],xhat,r)).astype(bf16)

def dx_rows(halves,x,dres,vec,pack1,blocks=3):
    t,d=x.shape; bs=t//blocks
    row=lambda n:pl.BlockSpec((bs,n),lambda i:(i,0))
    full=lambda s,**k:pl.BlockSpec(s,lambda i:(0,)*len(s),**k)
    return hbm_call(dx_kernel,grid=(blocks,),
        in_specs=[row(d//2)]*6+[row(d),row(d),full(vec.shape),full((16,192,1024),pipeline_mode=pl.Buffered(1))],
        out_specs=[row(d),full((8,d))],
        out_shape=[pltpu.HBM((t,d),bf16),pltpu.HBM((8,d),f32)],
        compiler_params=pltpu.CompilerParams(vmem_limit_bytes=48<<20),name="dx_rows",cost_estimate=cost(14))(*halves,x,dres,vec,pack1)

def grad_fc2_kernel(n_ref,dy_ref,out_ref):
    res=dot(n_ref[...],dy_ref[...],TN).astype(bf16)
    for f in range(out_ref.shape[0]):
        for r in range(8):
            out_ref[f,r]=res[256*f:256*f+256,128*r:128*r+128]

def grad_fc2(n,dy,steps=4):
    t,d=dy.shape; w=FF//steps
    return hbm_call(grad_fc2_kernel,grid=(steps,),
        in_specs=[pl.BlockSpec((t,w),lambda i:(0,i)),pl.BlockSpec((t,d),lambda i:(0,0),pipeline_mode=pl.Buffered(1))],
        out_specs=pl.BlockSpec((w//256,8,256,128),lambda i:(i,0,0,0)),
        out_shape=pltpu.HBM((16,8,256,128),bf16),
        compiler_params=pltpu.CompilerParams(vmem_limit_bytes=48<<20),name="grad_fc2",cost_estimate=cost(14))(n,dy)

def grad_up_kernel(c_ref,dz_ref,a2_ref,du_ref,out_ref,left):
    i=pl.program_id(0)
    def put(res):
        res=res.astype(bf16)
        for f in range(16):
            for r in range(8):
                out_ref[f,r]=res[64*f:64*f+64,128*r:128*r+128]
    @pl.when(i==0)
    def _():
        left[...]=c_ref[...].T
        put(dot(left[...],dz_ref[...]))
        left[...]=a2_ref[...].T
    @pl.when(i>0)
    def _(): put(dot(left[...],du_ref[...]))

def grad_up(c,dz,a2,du):
    t,d=c.shape
    full=pl.BlockSpec((t,d),lambda i:(0,0),pipeline_mode=pl.Buffered(1))
    return hbm_call(grad_up_kernel,grid=(5,),
        in_specs=[full,full,full,pl.BlockSpec((t,1024),lambda i:(0,jnp.maximum(i-1,0)))],
        out_specs=pl.BlockSpec((16,8,64,128),lambda i:(0,0,i,0)),
        out_shape=pltpu.HBM((16,8,320,128),bf16),
        scratch_shapes=[pltpu.VMEM((d,t),bf16)],
        compiler_params=pltpu.CompilerParams(vmem_limit_bytes=56<<20),name="grad_up",cost_estimate=cost(20))(c,dz,a2,du)

def grad_qkv_kernel(core_ref,a_ref,dq_ref,dk_ref,dv_ref,*refs):
    vecs,(keep_ref,give_ref)=refs[:-2],refs[-2:]
    i=pl.program_id(0)
    first=core_ref[0]==0
    for p,ref in enumerate((dq_ref,dk_ref,dv_ref)):
        res=dot(a_ref[...],ref[...],TN)
        for chip in range(2):
            even=res[128*chip:128*chip+64,:]; odd=res[128*chip+64:128*chip+128,:]
            mine=jnp.where(first,even,odd).astype(bf16)
            other=jnp.where(first,odd,even).astype(bf16)
            for l in range(4):
                for h in range(2):
                    q=2*(4*p+l)+h; at=32*(q%3)
                    keep_ref[q//3,chip,at:at+32,:]=mine[32*h:32*h+32,128*l:128*l+128]
                    give_ref[q//3,chip,at:at+32,:]=other[32*h:32*h+32,128*l:128*l+128]
    if vecs:
        b1_ref,b2_ref,gd_ref,gd0_ref,gf_ref=vecs
        for chip in range(2):
            cols=slice(128*chip,128*chip+128)
            half=jnp.where(i<2,b1_ref[:,cols],b2_ref[:,cols])
            line=lambda ref,k:ref[k:k+1,cols]
            ten=[jnp.zeros((2,128),f32),half,line(gd_ref,5),gd_ref[3:5,cols],gd_ref[1:3,cols],line(gd0_ref,0),line(gd_ref,6)]
            pick=lambda v,at:sum(jnp.where(i==k,gf_ref[4*v+k:4*v+k+1,at:at+128],0.0) for k in range(4))
            long=[pick(v,512*chip+128*b) for v in (2,0,1) for b in range(4)]
            rows=jnp.concatenate(ten+long+[jnp.zeros((1,128),f32)],axis=0).astype(bf16)
            for r in range(8):
                part=rows[8*r:8*r+8,:] if r<3 else jnp.zeros((8,128),bf16)
                keep_ref[r,chip,96:104,:]=part
                give_ref[r,chip,96:104,:]=part

def grad_qkv(core,a,dq,dk,dv,vecs=()):
    t,d=a.shape; w=dq.shape[1]; rows=104 if vecs else 96
    full=pl.BlockSpec((t,w),lambda i,c:(0,0),pipeline_mode=pl.Buffered(1))
    out=pl.BlockSpec((8,2,rows,128),lambda i,c:(0,i,0,0))
    lanes=lambda v:pl.BlockSpec((v.shape[0],256),lambda i,c:(0,i))
    more=[]
    if vecs:
        b1,b2,gd,gd0,gf=vecs
        half=lambda lo:pl.BlockSpec((2,256),lambda i,c:(0,jnp.clip(i-lo,0,1)))
        more=[half(0),half(2),lanes(gd),lanes(gd0),pl.BlockSpec(gf.shape,lambda i,c:(0,0))]
    return hbm_call(grad_qkv_kernel,
        grid_spec=pltpu.PrefetchScalarGridSpec(num_scalar_prefetch=1,grid=(4,),
            in_specs=[pl.BlockSpec((t,256),lambda i,c:(0,i)),full,full,full]+more,
            out_specs=[out,out]),
        out_shape=[pltpu.HBM((8,8,rows,128),bf16)]*2,
        compiler_params=pltpu.CompilerParams(vmem_limit_bytes=48<<20),name="grad_qkv",cost_estimate=cost(8))(core,a,dq,dk,dv,*vecs)

def totals_kernel(*refs):
    *parts,out_ref=refs
    at=0
    for p in parts:
        n=p.shape[1]
        total=jnp.sum(p[...].astype(f32),axis=0).astype(bf16)
        for r in range(8):
            out_ref[r,at:at+n,:]=total
        at+=n

def totals(parts):
    rows=sum(p.shape[1] for p in parts)
    return hbm_call(totals_kernel,out_shape=pltpu.HBM((8,rows,128),bf16),
        compiler_params=pltpu.CompilerParams(vmem_limit_bytes=40<<20),name="totals",cost_estimate=cost(4))(*parts)

def finish_kernel(core_ref,s_ref,qkv_ref,out_ref,fc1_ref,fc2_ref,ten_ref,three_ref):
    piece=lambda r,at,n:s_ref[r,at:at+n,:].astype(f32)
    for r in range(8):
        cols=slice(128*r,128*r+128)
        fc2_ref[:,cols]=piece(r,0,256)
        out_ref[:,cols]=piece(r,256,64)
        for j in range(4):
            fc1_ref[:,1024*j+128*r:1024*j+128*r+128]=piece(r,320+64*j,64)
    for half in range(2):
        for p in range(3):
            for l in range(4):
                lanes=1024*p+512*half+128*l
                for h in range(2):
                    q=2*(4*p+l)+h
                    qkv_ref[32*h:32*h+32,lanes:lanes+128]=piece(q//3,576+96*half+32*(q%3),32)
    first=core_ref[0]==0
    rows=jnp.concatenate([piece(r,768,8) for r in range(3)],axis=0)
    ten_ref[0:11,:]=jnp.where(first,rows[0:11,0:64],rows[0:11,64:128])
    ten_ref[11:16,:]=jnp.zeros((5,64),f32)
    for v in range(3):
        b=[rows[11+4*v+k:12+4*v+k,:] for k in range(4)]
        three_ref[v:v+1,0:128]=jnp.where(first,b[0],b[2])
        three_ref[v:v+1,128:256]=jnp.where(first,b[1],b[3])
    three_ref[3:8,:]=jnp.zeros((5,256),f32)

def finish(core,sums):
    sd=pltpu.HBM
    shapes=[(64,3072),(64,1024),(64,4096),(256,1024),(16,64),(8,256)]
    return hbm_call(finish_kernel,
        grid_spec=pltpu.PrefetchScalarGridSpec(num_scalar_prefetch=1,grid=(1,),
            in_specs=[pl.BlockSpec(sums.shape,lambda i,c:(0,0,0))],
            out_specs=[pl.BlockSpec(s,lambda i,c:(0,0)) for s in shapes]),
        out_shape=[sd(s,f32) for s in shapes],
        compiler_params=pltpu.CompilerParams(vmem_limit_bytes=40<<20),name="finish",cost_estimate=cost(5))(core,sums)

def pack_kernel(at_ref,*refs):
    *vecs,w_ref,out_ref=refs
    shard=at_ref[0]
    for j in range(3):
        out_ref[64*j:64*j+64,:]=w_ref[:,1024*j:1024*j+1024]
    lane=lax.broadcasted_iota(jnp.int32,(1,1024),1)
    rows=[]
    for r in vecs[:10]:
        v=r[...].astype(f32).reshape(1,-1)
        v=jnp.concatenate([v,v],axis=1)
        rows.append(jnp.where(lane//64==shard,jnp.concatenate([v]*8,axis=1),0.0))
    rows.append(jnp.where(lane//64==shard,jnp.broadcast_to(vecs[10][...].astype(f32).reshape(1,1),(1,1024)),0.0))
    for r in vecs[11:14]:
        v=jnp.concatenate([r[...].astype(f32).reshape(1,-1)]*4,axis=1)
        for j in range(4):
            rows.append(jnp.where(lane//256+4*j==shard,v,0.0))
    rows.append(jnp.zeros((1,1024),f32))
    out_ref[192:216,:]=jnp.concatenate(rows,axis=0).astype(bf16)

def pack_first(shard,vectors,w_qkv):
    full=lambda s:pl.BlockSpec(s,lambda i,c:(0,)*len(s))
    return hbm_call(pack_kernel,
        grid_spec=pltpu.PrefetchScalarGridSpec(num_scalar_prefetch=1,grid=(1,),
            in_specs=[full(v.shape) for v in vectors]+[full(w_qkv.shape)],out_specs=full((216,1024))),
        out_shape=pltpu.HBM((216,1024),bf16),name="pack_first",cost_estimate=cost(2))(shard,*vectors,w_qkv)

T=1152; D=1024
FWD_BLOCKS=[(0,384),(384,384),(768,384)]
BLOCKS=[(0,256),(256,256),(512,256),(768,256),(1024,128)]


def masked_scores(sT, start_row, q0, bq):
    keys=q0+bq
    kio=lax.broadcasted_iota(jnp.int32,(128,bq),0)
    qio=lax.broadcasted_iota(jnp.int32,(1,bq),1)+q0
    parts=[]
    for k0 in range(0,keys,128):
        t=sT[k0:k0+128]
        ok=None
        if k0==0 or q0+bq>1024:
            ok=kio>=start_row-k0
        if k0+127>q0:
            low=kio<=qio-k0
            ok=low if ok is None else ok&low
        parts.append(t if ok is None else jnp.where(ok,t,NEG))
    return jnp.concatenate(parts,axis=0) if len(parts)>1 else parts[0]

def fwd_kernel(start_ref,hs_ref,q_ref,k_ref,v_ref,o_ref,c_ref,lse_ref):
    lane=lax.broadcasted_iota(jnp.int32,(1,128),1)
    vT=v_ref[...].T
    oT=[]
    for q0,bq in FWD_BLOCKS:
        keys=q0+bq
        k=k_ref[0:keys,:]
        qb=q_ref[q0:q0+bq,:]*jnp.asarray(HD**-0.5,bf16)
        start=start_ref[0:1,q0:q0+bq]
        halves=[]
        for h in range(2):
            qh=jnp.where((lane>=64*h)&(lane<64*h+64),qb,jnp.zeros_like(qb))
            s=masked_scores(dot(k,qh,NT),start,q0,bq)
            m=jnp.max(s,axis=0,keepdims=True)
            e=jnp.exp(s-m)
            l=jnp.sum(e,axis=0,keepdims=True)
            lse_ref[0,h:h+1,q0:q0+bq]=m+jnp.log(l)
            oh=dot(vT[64*h:64*h+64,0:keys],e.astype(bf16))
            halves.append(oh*(1.0/l))
        o=jnp.concatenate(halves,axis=0).T
        o_ref[q0:q0+bq,:]=o
        c_ref[q0:q0+bq,:]=(o*hs_ref[10:11,:]).astype(bf16)

def attn_fwd(proj,start,hs_cols):
    return hbm_call(fwd_kernel,
        grid=(H//2,),
        in_specs=[pl.BlockSpec((1,T),lambda p:(0,0)),pl.BlockSpec((24,128),lambda p:(0,p)),
                  pl.BlockSpec((T,128),lambda p:(0,p)),pl.BlockSpec((T,128),lambda p:(0,8+p)),pl.BlockSpec((T,128),lambda p:(0,16+p))],
        out_specs=[pl.BlockSpec((T,128),lambda p:(0,p)),pl.BlockSpec((T,128),lambda p:(0,p)),pl.BlockSpec((1,2,T),lambda p:(p,0,0))],
        out_shape=[pltpu.HBM((T,D),f32),pltpu.HBM((T,D),bf16),pltpu.HBM((H//2,2,T),f32)],
        compiler_params=pltpu.CompilerParams(vmem_limit_bytes=48<<20),
        name="attn_fwd",cost_estimate=cost(40))(start,hs_cols,proj,proj,proj)

def bwd_kernel(start_ref,lse_ref,o_ref,q_ref,k_ref,v_ref,do_ref,dq_ref,dk_ref,dv_ref,bsum_ref,dk_acc,dv_acc,dqT):
    lane=lax.broadcasted_iota(jnp.int32,(1,128),1)
    scale=jnp.asarray(HD**-0.5,bf16)
    kT=(k_ref[...]*scale).T
    prodT=(o_ref[...]*do_ref[...].astype(f32)).T
    delta=[jnp.sum(prodT[64*h:64*h+64],axis=0,keepdims=True) for h in range(2)]
    dk_acc[...]=jnp.zeros_like(dk_acc)
    dv_acc[...]=jnp.zeros_like(dv_acc)
    for q0,bq in BLOCKS:
        keys=q0+bq
        k=k_ref[0:keys,:]
        v=v_ref[0:keys,:]
        qb=q_ref[q0:q0+bq,:]*scale
        dob=do_ref[q0:q0+bq,:]
        start=start_ref[0:1,q0:q0+bq]
        for h in range(2):
            half=(lane>=64*h)&(lane<64*h+64)
            qh=jnp.where(half,qb,jnp.zeros_like(qb))
            doh=jnp.where(half,dob,jnp.zeros_like(dob))
            s=masked_scores(dot(k,qh,NT),start,q0,bq)
            p=jnp.exp(s-lse_ref[0,h:h+1,q0:q0+bq])
            dp=dot(v,doh,NT)
            ds=(p*(dp-delta[h][:,q0:q0+bq])).astype(bf16)
            dv_acc[0:keys,:]+=dot(p.astype(bf16),doh)
            dk_acc[0:keys,:]+=dot(ds,qh)
            dqT[64*h:64*h+64,q0:q0+bq]=dot(kT[64*h:64*h+64,0:keys],ds)
    dq=dqT[...].T.astype(bf16)
    dk=dk_acc[...].astype(bf16)
    dv=dv_acc[...].astype(bf16)
    dq_ref[...]=dq; dk_ref[...]=dk; dv_ref[...]=dv
    bsum_ref[0:1,:]=jnp.sum(dq.astype(f32),axis=0,keepdims=True)
    bsum_ref[1:2,:]=jnp.sum(dv.astype(f32),axis=0,keepdims=True)

def attn_bwd(proj,start,lse,o,do,half):
    pairs=H//4; at=half*pairs
    blk=lambda off:pl.BlockSpec((T,128),lambda p:(0,off+at+p))
    out=pl.BlockSpec((T,128),lambda p:(0,p))
    return hbm_call(bwd_kernel,
        grid=(pairs,),
        in_specs=[pl.BlockSpec((1,T),lambda p:(0,0)),pl.BlockSpec((1,2,T),lambda p:(at+p,0,0)),blk(0),blk(0),blk(8),blk(16),blk(0)],
        out_specs=[out,out,out,pl.BlockSpec((2,128),lambda p:(0,p))],
        out_shape=[pltpu.HBM((T,D//2),bf16)]*3+[pltpu.HBM((2,D//2),f32)],
        scratch_shapes=[pltpu.VMEM((T,128),f32),pltpu.VMEM((T,128),f32),pltpu.VMEM((128,T),f32)],
        compiler_params=pltpu.CompilerParams(vmem_limit_bytes=48<<20),
        name="attn_bwd",cost_estimate=cost(20))(start,lse,o,proj,proj,proj,do)

EVERY = ("replica", "chip", "core")
SHARD = ("chip", "core")
PEERS = ("replica", "chip")


def exchange(slab, devices):
    return lax.all_to_all(slab.reshape(devices, -1, 128), EVERY, split_axis=0, concat_axis=0, tiled=True).reshape(-1, 128)


def replica_parts(part):
    return lax.all_to_all(part, "replica", split_axis=0, concat_axis=0, tiled=True)


def core_sum(keep, give):
    taken = lax.ppermute(give, "core", [(0, 1), (1, 0)])
    both = keep.astype(f32) + taken.astype(f32)
    return both.astype(bf16).reshape(64, *keep.shape[2:])


def peer_parts(both):
    return lax.all_to_all(both, PEERS, split_axis=0, concat_axis=0, tiled=True)


def on_device(
    tokens, cotangent, lengths, deal_order, inverse, ln1_gain, ln1_bias, w_qkv, b_query, b_value, head_scale, w_out, b_out,
    post_gain, post_bias, ln2_gain, ln2_bias, w_fc1, b_fc1, ffn_gain, ffn_bias, w_fc2, b_fc2,
):
    devices = lax.axis_size(EVERY)
    replicas = lax.axis_size("replica")
    count, width = tokens.shape
    core = lax.axis_index("core").astype(jnp.int32).reshape(1)
    shard = lax.axis_index(SHARD).astype(jnp.int32).reshape(1)
    vectors = [ln1_gain, ln1_bias, b_query, b_value, b_out, post_gain, post_bias, ln2_gain, ln2_bias, b_fc2, head_scale,
               b_fc1, ffn_gain, ffn_bias]
    first = pack_first(shard, vectors, w_qkv)
    pack1 = lax.all_gather(first, SHARD, axis=0)
    recv_keys = deal_order // count * count + jnp.arange(count, dtype=jnp.int32)
    first, tokens = lax.optimization_barrier((first, tokens))
    sent_x = send_rows(tokens, inverse)
    got_x = exchange(sent_x, devices)
    sent_x, w_out, w_fc1, cotangent = lax.optimization_barrier((sent_x, w_out, w_fc1, cotangent))
    packa = lax.all_gather(jnp.concatenate([w_out] + [w_fc1[:, width * j : width * j + width] for j in range(4)], axis=0), SHARD, axis=0)
    packb = lax.all_gather(w_fc2, SHARD, axis=0)
    sent_dy = send_rows(cotangent, inverse)
    sent_dy, got_x, pack1 = lax.optimization_barrier((sent_dy, got_x, pack1))
    got_dy = exchange(sent_dy, devices)
    vec = jnp.sum(pack1[:, 192:216].astype(f32), axis=0)
    places = jnp.arange(count, dtype=jnp.int32)
    starts = jnp.zeros((count,), jnp.int32)
    seq_end = jnp.zeros((), jnp.int32)
    for i in range(lengths.shape[1]):
        seq_end = seq_end + lengths[0, i]
        starts = jnp.where(places >= seq_end, seq_end, starts)
    starts = starts.reshape(1, count)
    x_rows, a, proj = recv_qkv(got_x, recv_keys, vec, pack1)
    o, c, lse = attn_fwd(proj, starts, vec)
    got_dy, c = lax.optimization_barrier((got_dy, c))
    dy_rows = recv_rows(got_dy, recv_keys)
    a2, n, vhat, gp, hres, zhat, stats = up_rows(c, x_rows, vec, packa)
    grads_fc2 = grad_fc2(n, dy_rows)
    grads_fc2, gp = lax.optimization_barrier((grads_fc2, gp))
    part_fc2 = lax.psum_scatter(grads_fc2, SHARD, scatter_dimension=0)
    y, du, gd0, gf = down_rows(n, vhat, gp, stats, dy_rows, hres, vec, packb)
    sent_y = send_rows(y, recv_keys)
    sent_y, du = lax.optimization_barrier((sent_y, du))
    got_y = exchange(sent_y, devices)
    dz, do, dres, gd = back_rows(du, dy_rows, hres, zhat, stats, o, vec, packa)
    grads_up = grad_up(c, dz, a2, du)
    grads_up, do, got_y = lax.optimization_barrier((grads_up, do, got_y))
    grads_up, part_fc2 = lax.optimization_barrier((grads_up, part_fc2))
    part_up = lax.psum_scatter(grads_up, SHARD, scatter_dimension=0)
    parts_fc2 = replica_parts(part_fc2)
    halves1 = attn_bwd(proj, starts, lse, o, do, 0)
    dq1, parts_fc2 = lax.optimization_barrier((halves1[0], parts_fc2))
    both1 = core_sum(*grad_qkv(core, a, dq1, *halves1[1:3]))
    parts1 = peer_parts(both1)
    both1, do = lax.optimization_barrier((both1, do))
    halves2 = attn_bwd(proj, starts, lse, o, do, 1)
    dq2, parts1 = lax.optimization_barrier((halves2[0], parts1))
    both2 = core_sum(*grad_qkv(core, a, dq2, *halves2[1:3], (halves1[3], halves2[3], gd, gd0, gf)))
    parts2 = peer_parts(both2)
    both2, dq2 = lax.optimization_barrier((both2, dq2))
    dx, gl = dx_rows([dq1, *halves1[1:3], dq2, *halves2[1:3]], x_rows, dres, vec, pack1)
    sent_dx = send_more(dx, recv_keys, gl)
    sent_dx, parts2, part_up = lax.optimization_barrier((sent_dx, parts2, part_up))
    parts_up = replica_parts(part_up)
    sent_dx, parts_up = lax.optimization_barrier((sent_dx, parts_up))
    got_dx = lax.all_to_all(sent_dx, EVERY, split_axis=0, concat_axis=0, tiled=True)
    parts_up, got_y, sent_dx = lax.optimization_barrier((parts_up, got_y, sent_dx))
    output = recv_rows(got_y, inverse)
    spread = totals([parts_fc2, parts_up, parts1, parts2])
    spread, got_dx, output = lax.optimization_barrier((spread, got_dx, output))
    sums = lax.all_to_all(spread, "replica", split_axis=0, concat_axis=0, tiled=True)
    grad_tokens, g_ln1 = recv_more(got_dx, inverse)
    g_ln1 = jnp.where(core[0] == 0, g_ln1[0:2, 0:64], g_ln1[0:2, 64:128])
    g_qkv, g_out, g_fc1, g_fc2, ten, three = finish(core, sums)
    v = [ten[k] for k in range(10)]
    return (
        output, grad_tokens, g_ln1[0], g_ln1[1], g_qkv, v[2], v[3], jnp.sum(ten[10]).reshape(1), g_out, v[4], v[5], v[6], v[7], v[8], g_fc1,
        three[0], three[1], three[2], g_fc2, v[9],
    )


def solution(mesh):
    replicas, shards = mesh.devices.shape
    mesh = jax.sharding.Mesh(mesh.devices.reshape(replicas, shards // 2, 2), EVERY)
    rows, vector, matrix = P(EVERY, None), P(SHARD), P(SHARD, None)
    in_specs = (
        rows, rows, rows, P(EVERY), P(EVERY), vector, vector, matrix, vector, vector, vector, matrix, vector, vector, vector,
        vector, vector, matrix, vector, vector, vector, matrix, vector,
    )
    out_specs = (
        rows, rows, vector, vector, matrix, vector, vector, vector, matrix, vector, vector, vector, vector, vector, matrix,
        vector, vector, vector, matrix, vector,
    )
    return jax.shard_map(on_device, mesh=mesh, in_specs=in_specs, out_specs=out_specs, check_vma=False)
```

```python
import jax
import jax.numpy as jnp
from jax import lax
from jax.experimental import pallas as pl
from jax.experimental.pallas import tpu as pltpu
from jax.sharding import PartitionSpec as P

f32 = jnp.float32
bf16 = jnp.bfloat16
H = 16
HD = 64
EPS = 1e-5
NEG = -1000000000.0
NT = (((1,), (1,)), ((), ()))
NN = (((1,), (0,)), ((), ()))
TN = (((0,), (0,)), ((), ()))


def dot(a, b, dn=NN):
    return lax.dot_general(a, b, dn, preferred_element_type=f32)


def hbm_call(kernel, **kw):
    call = pl.pallas_call(kernel, **kw)
    pin = lambda v: pltpu.with_memory_space_constraint(v, pltpu.HBM) if v.size > 1000 else v
    return lambda *args: call(*[pin(v) for v in args])


def cost(micros):
    return pl.CostEstimate(flops=0, transcendentals=0, bytes_accessed=micros * 3000000)

def rank_row(kcol,krow):
    return jnp.sum((kcol<krow).astype(f32),axis=0,keepdims=True).astype(jnp.int32)
def rank_col(krow,kcol):
    return jnp.sum((krow<kcol).astype(f32),axis=1,keepdims=True).astype(jnp.int32)

def send_kernel(krow_ref,kcol_ref,x_ref,out_ref,rank_ref,wide_ref):
    i=pl.program_id(0); bs=out_ref.shape[0]//8
    @pl.when(i==0)
    def _(): rank_ref[...]=rank_row(kcol_ref[...],krow_ref[...])
    t=rank_ref.shape[1]
    pick=(lax.broadcasted_iota(jnp.int32,(bs,t),0)+i*bs==rank_ref[...]).astype(f32).astype(bf16)
    rows=dot(pick,x_ref[...])
    for k in range(8):
        wide_ref[pl.ds(k,bs,stride=8),:]=rows[:,128*k:128*k+128]
    out_ref[...]=wide_ref[...].astype(bf16)

def send_rows(x,keys,blocks=3):
    t,d=x.shape; bs=t//blocks
    full=lambda s:pl.BlockSpec(s,lambda i:(0,0))
    return hbm_call(send_kernel,grid=(blocks,),
        in_specs=[full((1,t)),full((t,1)),full((t,d))],
        out_specs=pl.BlockSpec((bs*8,128),lambda i:(i,0)),
        out_shape=pltpu.HBM((t*8,128),bf16),
        scratch_shapes=[pltpu.VMEM((1,t),jnp.int32),pltpu.VMEM((bs*8,128),f32)],
        compiler_params=pltpu.CompilerParams(vmem_limit_bytes=40<<20),name="send_rows",cost_estimate=cost(5))(keys.reshape(1,t),keys.reshape(t,1),x)

def unpack_rows(got_ref,wide_ref,rows_ref,chunk=384):
    t=rows_ref.shape[0]
    for c in range(0,t,chunk):
        wide_ref[...]=got_ref[8*c:8*(c+chunk),:].astype(f32)
        for k in range(8):
            rows_ref[c:c+chunk,128*k:128*k+128]=wide_ref[pl.ds(k,chunk,stride=8),:].astype(bf16)

def recv_kernel(krow_ref,kcol_ref,got_ref,out_ref,wide_ref,rows_ref):
    i=pl.program_id(0); bs=out_ref.shape[0]
    @pl.when(i==0)
    def _(): unpack_rows(got_ref,wide_ref,rows_ref)
    t=rows_ref.shape[0]
    rank=rank_col(krow_ref[...],kcol_ref[...])
    pick=(lax.broadcasted_iota(jnp.int32,(bs,t),1)==rank).astype(f32).astype(bf16)
    out_ref[...]=dot(pick,rows_ref[...]).astype(bf16)

def recv_rows(got,keys,blocks=3):
    t=got.shape[0]//8; d=1024; bs=t//blocks
    full=lambda s:pl.BlockSpec(s,lambda i:(0,0))
    return hbm_call(recv_kernel,grid=(blocks,),
        in_specs=[full((1,t)),pl.BlockSpec((bs,1),lambda i:(i,0)),full((t*8,128))],
        out_specs=pl.BlockSpec((bs,d),lambda i:(i,0)),
        out_shape=pltpu.HBM((t,d),bf16),
        scratch_shapes=[pltpu.VMEM((384*8,128),f32),pltpu.VMEM((t,d),bf16)],
        compiler_params=pltpu.CompilerParams(vmem_limit_bytes=40<<20),name="recv_rows",cost_estimate=cost(6))(keys.reshape(1,t),keys.reshape(t,1),got)

def recv_more_kernel(krow_ref,kcol_ref,got_ref,out_ref,more_ref,wide_ref,rows_ref):
    i=pl.program_id(0); bs=out_ref.shape[0]; t=rows_ref.shape[0]
    @pl.when(i==0)
    def _():
        for c in range(0,t,288):
            wide_ref[...]=got_ref[c//9:c//9+32,0:72,:].reshape(288*8,128).astype(f32)
            for k in range(8):
                rows_ref[c:c+288,128*k:128*k+128]=wide_ref[pl.ds(k,288,stride=8),:].astype(bf16)
        more_ref[...]=jnp.sum(got_ref[:,72:80,:].astype(f32),axis=0)
    rank=rank_col(krow_ref[...],kcol_ref[...])
    pick=(lax.broadcasted_iota(jnp.int32,(bs,t),1)==rank).astype(f32).astype(bf16)
    out_ref[...]=dot(pick,rows_ref[...]).astype(bf16)

def recv_more(got,keys,blocks=3):
    t=got.shape[0]*9; d=1024; bs=t//blocks
    full=lambda s:pl.BlockSpec(s,lambda i:(0,)*len(s))
    return hbm_call(recv_more_kernel,grid=(blocks,),
        in_specs=[full((1,t)),pl.BlockSpec((bs,1),lambda i:(i,0)),full(got.shape)],
        out_specs=[pl.BlockSpec((bs,d),lambda i:(i,0)),full((8,128))],
        out_shape=[pltpu.HBM((t,d),bf16),pltpu.HBM((8,128),f32)],
        scratch_shapes=[pltpu.VMEM((288*8,128),f32),pltpu.VMEM((t,d),bf16)],
        compiler_params=pltpu.CompilerParams(vmem_limit_bytes=40<<20),name="recv_more",cost_estimate=cost(6))(keys.reshape(1,t),keys.reshape(t,1),got)

def norm_parts(v):
    m=jnp.mean(v,axis=-1,keepdims=True); c=v-m
    r=lax.rsqrt(jnp.mean(c*c,axis=-1,keepdims=True)+EPS)
    return c*r,r
def norm_back(e,g,vhat,r):
    eg=e*g
    return r*(eg-jnp.mean(eg,axis=-1,keepdims=True)-vhat*jnp.mean(eg*vhat,axis=-1,keepdims=True))
def colsum(v): return jnp.sum(v,axis=0,keepdims=True)

def qkv_kernel(krow_ref,kcol_ref,got_ref,vec_ref,w_ref,x_ref,a_ref,proj_ref,wide_ref,rows_ref):
    i=pl.program_id(0); bs=x_ref.shape[0]
    @pl.when(i==0)
    def _(): unpack_rows(got_ref,wide_ref,rows_ref)
    t=rows_ref.shape[0]
    rank=rank_col(krow_ref[...],kcol_ref[...])
    pick=(lax.broadcasted_iota(jnp.int32,(bs,t),1)==rank).astype(f32).astype(bf16)
    x=dot(pick,rows_ref[...])
    x_ref[...]=x.astype(bf16)
    xhat,_=norm_parts(x)
    a=(xhat*vec_ref[0:1,:]+vec_ref[1:2,:]).astype(bf16)
    a_ref[...]=a
    for j in range(3):
        w=w_ref[:,64*j:64*j+64,:].reshape(1024,1024)
        pj=dot(a,w)
        if j==0: pj=pj+vec_ref[2:3,:]
        if j==2: pj=pj+vec_ref[3:4,:]
        proj_ref[:,1024*j:1024*j+1024]=pj.astype(bf16)

def recv_qkv(got,keys,vec,pack1,blocks=3):
    t=got.shape[0]//8; d=1024; bs=t//blocks
    full=lambda s:pl.BlockSpec(s,lambda i:(0,)*len(s))
    return hbm_call(qkv_kernel,grid=(blocks,),
        in_specs=[full((1,t)),pl.BlockSpec((bs,1),lambda i:(i,0)),full((t*8,128)),full(vec.shape),
                  pl.BlockSpec((16,192,1024),lambda i:(0,0,0),pipeline_mode=pl.Buffered(1))],
        out_specs=[pl.BlockSpec((bs,d),lambda i:(i,0)),pl.BlockSpec((bs,d),lambda i:(i,0)),pl.BlockSpec((bs,3*d),lambda i:(i,0))],
        out_shape=[pltpu.HBM((t,d),bf16),pltpu.HBM((t,d),bf16),pltpu.HBM((t,3*d),bf16)],
        scratch_shapes=[pltpu.VMEM((384*8,128),f32),pltpu.VMEM((t,d),bf16)],
        compiler_params=pltpu.CompilerParams(vmem_limit_bytes=48<<20),name="recv_qkv",cost_estimate=cost(18))(keys.reshape(1,t),keys.reshape(t,1),got,vec,pack1)

RT2=0.7071067811865476; RPI=0.3989422804014327
FF=4096
def up_kernel(c_ref,x_ref,vec_ref,w_ref,a2_ref,n_ref,vhat_ref,gp_ref,hres_ref,zhat_ref,st_ref,g_s):
    vec=lambda k:vec_ref[k:k+1,:]
    z=dot(c_ref[...],w_ref[:,0:64,:].reshape(1024,1024))+vec(4)
    zhat,rz=norm_parts(z)
    zhat_ref[...]=zhat
    hres=x_ref[...].astype(f32)+zhat*vec(5)+vec(6)
    hres_ref[...]=hres
    hhat,_=norm_parts(hres)
    a2=(hhat*vec(7)+vec(8)).astype(bf16)
    a2_ref[...]=a2
    tot=0.0
    for j in range(4):
        cols=slice(1024*j,1024*j+1024)
        u=dot(a2,w_ref[:,64+64*j:128+64*j,:].reshape(1024,1024))+vec(11+j)
        phi=0.5+0.5*lax.erf(u*RT2)
        g=u*phi
        gp_ref[:,cols]=(phi+u*(RPI*jnp.exp(-0.5*u*u))).astype(bf16)
        g_s[:,cols]=g
        tot=tot+jnp.sum(g,axis=-1,keepdims=True)
    mean=tot*(1.0/FF)
    var=0.0
    for j in range(4):
        cen=g_s[:,1024*j:1024*j+1024]-mean
        var=var+jnp.sum(cen*cen,axis=-1,keepdims=True)
    rf=lax.rsqrt(var*(1.0/FF)+EPS)
    for j in range(4):
        cols=slice(1024*j,1024*j+1024)
        vhat=(g_s[:,cols]-mean)*rf
        vhat_ref[:,cols]=vhat.astype(bf16)
        n_ref[:,cols]=(vhat*vec(15+j)+vec(19+j)).astype(bf16)
    lane=lax.broadcasted_iota(jnp.int32,(1,128),1)
    st_ref[...]=jnp.where(lane==0,rz,rf)

def row_specs(bm):
    row=lambda n:pl.BlockSpec((bm,n),lambda i:(i,0))
    full=lambda s,**k:pl.BlockSpec(s,lambda i:(0,)*len(s),**k)
    return row,full

def up_rows(c,x,vec,packa,bm=384):
    t,d=c.shape
    row,full=row_specs(bm); sd=pltpu.HBM
    return hbm_call(up_kernel,grid=(t//bm,),
        in_specs=[row(d),row(d),full(vec.shape),full(packa.shape,pipeline_mode=pl.Buffered(1))],
        out_specs=[row(d),row(FF),row(FF),row(FF),row(d),row(d),row(128)],
        out_shape=[sd((t,d),bf16),sd((t,FF),bf16),sd((t,FF),bf16),sd((t,FF),bf16),sd((t,d),f32),sd((t,d),f32),sd((t,128),f32)],
        scratch_shapes=[pltpu.VMEM((bm,FF),f32)],
        compiler_params=pltpu.CompilerParams(vmem_limit_bytes=60<<20),name="up_rows",cost_estimate=cost(45))(c,x,vec,packa)

def down_kernel(n_ref,vhat_ref,gp_ref,st_ref,dy_ref,hres_ref,vec_ref,w_ref,krow_ref,kcol_ref,out_ref,du_ref,gd_ref,gf_ref,e_s,y_s,rank_ref,wide_ref):
    i=pl.program_id(0); steps=4; bs=dy_ref.shape[0]
    @pl.when(i==0)
    def _():
        gd_ref[...]=jnp.zeros_like(gd_ref); gf_ref[...]=jnp.zeros_like(gf_ref)
        rank_ref[...]=rank_row(kcol_ref[...],krow_ref[...])
    @pl.when(i<steps)
    def _():
        vec=lambda k:vec_ref[k:k+1,:]
        rf=st_ref[:,1:2]
        dy=dy_ref[...]
        w=lambda j:w_ref[4*j:4*j+4].reshape(1024,1024)
        s1=0.0; s2=0.0
        dn=dot(dy,w(0),NT)
        for j in range(4):
            cols=slice(1024*j,1024*j+1024)
            ahead=dot(dy,w(j+1),NT) if j<3 else None
            dv=dn*vhat_ref[:,cols].astype(f32)
            gf_ref[j:j+1,:]+=colsum(dv)
            gf_ref[4+j:5+j,:]+=colsum(dn)
            gain=vec(15+j)
            e=dn*gain
            e_s[:,cols]=e
            s1=s1+jnp.sum(e,axis=-1,keepdims=True)
            s2=s2+jnp.sum(dv*gain,axis=-1,keepdims=True)
            dn=ahead
        s1=rf*s1*(1.0/FF); s2=rf*s2*(1.0/FF)
        y=hres_ref[...]+vec(9)
        for j in range(4):
            cols=slice(1024*j,1024*j+1024)
            y=y+dot(n_ref[:,cols],w(j))
            du=gp_ref[:,cols].astype(f32)*(rf*e_s[:,cols]-s1-vhat_ref[:,cols].astype(f32)*s2)
            du_ref[:,cols]=du.astype(bf16)
            gf_ref[8+j:9+j,:]+=colsum(du)
        y_s[pl.ds(pl.multiple_of(i*bs,bs),bs),:]=y.astype(bf16)
        gd_ref[0:1,:]+=colsum(dy.astype(f32))
    @pl.when(i>=steps)
    def _():
        n=out_ref.shape[0]//8; t=rank_ref.shape[1]
        pick=(lax.broadcasted_iota(jnp.int32,(n,t),0)+(i-steps)*n==rank_ref[...]).astype(f32).astype(bf16)
        rows=dot(pick,y_s[...])
        for k in range(8):
            wide_ref[pl.ds(k,n,stride=8),:]=rows[:,128*k:128*k+128]
        out_ref[...]=wide_ref[...].astype(bf16)

def down_rows(n,vhat,gp,st,dy,hres,vec,packb,keys):
    t,d=dy.shape; bm=t//4
    row=lambda n:pl.BlockSpec((bm,n),lambda i:(jnp.minimum(i,3),0))
    full=lambda s,**k:pl.BlockSpec(s,lambda i:(0,)*len(s),**k)
    sd=pltpu.HBM
    return hbm_call(down_kernel,grid=(7,),
        in_specs=[row(FF),row(FF),row(FF),row(128),row(d),row(d),full(vec.shape),full(packb.shape,pipeline_mode=pl.Buffered(1)),full((1,t)),full((t,1))],
        out_specs=[pl.BlockSpec((t//3*8,128),lambda i:(jnp.maximum(i-4,0),0)),row(FF),full((8,d)),full((16,d))],
        out_shape=[sd((t*8,128),bf16),sd((t,FF),bf16),sd((8,d),f32),sd((16,d),f32)],
        scratch_shapes=[pltpu.VMEM((bm,FF),f32),pltpu.VMEM((t,d),bf16),pltpu.VMEM((1,t),jnp.int32),pltpu.VMEM((t//3*8,128),f32)],
        compiler_params=pltpu.CompilerParams(vmem_limit_bytes=60<<20),name="down_rows",cost_estimate=cost(40))(n,vhat,gp,st,dy,hres,vec,packb,keys.reshape(1,t),keys.reshape(t,1))

def back_kernel(du_ref,dy_ref,hres_ref,zhat_ref,st_ref,o_ref,vec_ref,w_ref,dz_ref,do_ref,dres_ref,gd_ref):
    @pl.when(pl.program_id(0)==0)
    def _(): gd_ref[...]=jnp.zeros_like(gd_ref)
    vec=lambda k:vec_ref[k:k+1,:]
    da2=0.0
    for j in range(4):
        da2=da2+dot(du_ref[:,1024*j:1024*j+1024],w_ref[:,64+64*j:128+64*j,:].reshape(1024,1024),NT)
    hhat,rh=norm_parts(hres_ref[...])
    gd_ref[1:2,:]+=colsum(da2*hhat)
    gd_ref[2:3,:]+=colsum(da2)
    dres=dy_ref[...].astype(f32)+norm_back(da2,vec(7),hhat,rh)
    dres_ref[...]=dres
    zhat=zhat_ref[...]
    gd_ref[3:4,:]+=colsum(dres*zhat)
    gd_ref[4:5,:]+=colsum(dres)
    dz=norm_back(dres,vec(5),zhat,st_ref[:,0:1]).astype(bf16)
    dz_ref[...]=dz
    gd_ref[5:6,:]+=colsum(dz.astype(f32))
    dc=dot(dz,w_ref[:,0:64,:].reshape(1024,1024),NT)
    gd_ref[6:7,:]+=colsum(dc*o_ref[...])
    do_ref[...]=(dc*vec(10)).astype(bf16)

def back_rows(du,dy,hres,zhat,st,o,vec,packa,bm=288):
    t,d=dy.shape
    row,full=row_specs(bm); sd=pltpu.HBM
    return hbm_call(back_kernel,grid=(t//bm,),
        in_specs=[row(FF),row(d),row(d),row(d),row(128),row(d),full(vec.shape),full(packa.shape,pipeline_mode=pl.Buffered(1))],
        out_specs=[row(d),row(d),row(d),full((8,d))],
        out_shape=[sd((t,d),bf16),sd((t,d),bf16),sd((t,d),f32),sd((8,d),f32)],
        compiler_params=pltpu.CompilerParams(vmem_limit_bytes=60<<20),name="back_rows",cost_estimate=cost(25))(du,dy,hres,zhat,st,o,vec,packa)

def dx_send_kernel(*refs):
    *halves,x_ref,dres_ref,vec_ref,w_ref,krow_ref,kcol_ref,out_ref,g_s,dx_s,rank_ref,wide_ref=refs
    i=pl.program_id(0); steps=3
    @pl.when(i==0)
    def _():
        g_s[...]=jnp.zeros_like(g_s)
        rank_ref[...]=rank_row(kcol_ref[...],krow_ref[...])
    @pl.when(i<steps)
    def _():
        bs=x_ref.shape[0]
        da=0.0
        for j in range(3):
            w=w_ref[:,64*j:64*j+64,:].reshape(1024,1024)
            da=da+dot(halves[j][...],w[:,0:512],NT)+dot(halves[3+j][...],w[:,512:1024],NT)
        xhat,r=norm_parts(x_ref[...].astype(f32))
        g_s[0:1,:]+=colsum(da*xhat)
        g_s[1:2,:]+=colsum(da)
        dx_s[pl.ds(pl.multiple_of(i*bs,bs),bs),:]=(dres_ref[...]+norm_back(da,vec_ref[0:1,:],xhat,r)).astype(bf16)
    @pl.when(i>=steps)
    def _():
        slabs=out_ref.shape[0]; bs=slabs*9; t=rank_ref.shape[1]
        pick=(lax.broadcasted_iota(jnp.int32,(bs,t),0)+(i-steps)*bs==rank_ref[...]).astype(f32).astype(bf16)
        rows=dot(pick,dx_s[...])
        for k in range(8):
            wide_ref[pl.ds(k,bs,stride=8),:]=rows[:,128*k:128*k+128]
        out_ref[:,0:72,:]=wide_ref[...].astype(bf16).reshape(slabs,72,128)
        more=g_s[...].astype(bf16)
        for d in range(slabs):
            chip=d%16//2
            out_ref[d,72:80,:]=more[:,128*chip:128*chip+128]

def dx_send(halves,x,dres,vec,pack1,keys):
    t,d=x.shape; bs=t//3
    row=lambda n:pl.BlockSpec((bs,n),lambda i:(jnp.minimum(i,2),0))
    full=lambda s,**k:pl.BlockSpec(s,lambda i:(0,)*len(s),**k)
    return hbm_call(dx_send_kernel,grid=(7,),
        in_specs=[row(d//2)]*6+[row(d),row(d),full(vec.shape),full((16,192,1024),pipeline_mode=pl.Buffered(1)),full((1,t)),full((t,1))],
        out_specs=pl.BlockSpec((t//36,80,128),lambda i:(jnp.maximum(i-3,0),0,0)),
        out_shape=pltpu.HBM((t//9,80,128),bf16),
        scratch_shapes=[pltpu.VMEM((8,d),f32),pltpu.VMEM((t,d),bf16),pltpu.VMEM((1,t),jnp.int32),pltpu.VMEM((t//4*8,128),f32)],
        compiler_params=pltpu.CompilerParams(vmem_limit_bytes=48<<20),name="dx_send",cost_estimate=cost(18))(*halves,x,dres,vec,pack1,keys.reshape(1,t),keys.reshape(t,1))

def grad_fc2_kernel(n_ref,dy_ref,out_ref):
    res=dot(n_ref[...],dy_ref[...],TN).astype(bf16)
    for f in range(out_ref.shape[0]):
        for r in range(8):
            out_ref[f,r]=res[256*f:256*f+256,128*r:128*r+128]

def grad_fc2(n,dy,steps=4):
    t,d=dy.shape; w=FF//steps
    return hbm_call(grad_fc2_kernel,grid=(steps,),
        in_specs=[pl.BlockSpec((t,w),lambda i:(0,i)),pl.BlockSpec((t,d),lambda i:(0,0),pipeline_mode=pl.Buffered(1))],
        out_specs=pl.BlockSpec((w//256,8,256,128),lambda i:(i,0,0,0)),
        out_shape=pltpu.HBM((16,8,256,128),bf16),
        compiler_params=pltpu.CompilerParams(vmem_limit_bytes=48<<20),name="grad_fc2",cost_estimate=cost(14))(n,dy)

def grad_up_kernel(c_ref,dz_ref,a2_ref,du_ref,out_ref,left):
    i=pl.program_id(0)
    def put(res):
        res=res.astype(bf16)
        for f in range(16):
            for r in range(8):
                out_ref[f,r]=res[64*f:64*f+64,128*r:128*r+128]
    @pl.when(i==0)
    def _():
        left[...]=c_ref[...].T
        put(dot(left[...],dz_ref[...]))
        left[...]=a2_ref[...].T
    @pl.when(i>0)
    def _(): put(dot(left[...],du_ref[...]))

def grad_up(c,dz,a2,du):
    t,d=c.shape
    full=pl.BlockSpec((t,d),lambda i:(0,0),pipeline_mode=pl.Buffered(1))
    return hbm_call(grad_up_kernel,grid=(5,),
        in_specs=[full,full,full,pl.BlockSpec((t,1024),lambda i:(0,jnp.maximum(i-1,0)))],
        out_specs=pl.BlockSpec((16,8,64,128),lambda i:(0,0,i,0)),
        out_shape=pltpu.HBM((16,8,320,128),bf16),
        scratch_shapes=[pltpu.VMEM((d,t),bf16)],
        compiler_params=pltpu.CompilerParams(vmem_limit_bytes=56<<20),name="grad_up",cost_estimate=cost(20))(c,dz,a2,du)

def grad_qkv_kernel(core_ref,a_ref,dq_ref,dk_ref,dv_ref,*refs):
    vecs,(keep_ref,give_ref)=refs[:-2],refs[-2:]
    i=pl.program_id(0)
    first=core_ref[0]==0
    for p,ref in enumerate((dq_ref,dk_ref,dv_ref)):
        res=dot(a_ref[...],ref[...],TN)
        for chip in range(2):
            even=res[128*chip:128*chip+64,:]; odd=res[128*chip+64:128*chip+128,:]
            mine=jnp.where(first,even,odd).astype(bf16)
            other=jnp.where(first,odd,even).astype(bf16)
            for l in range(4):
                for h in range(2):
                    q=2*(4*p+l)+h; at=32*(q%3)
                    keep_ref[q//3,chip,at:at+32,:]=mine[32*h:32*h+32,128*l:128*l+128]
                    give_ref[q//3,chip,at:at+32,:]=other[32*h:32*h+32,128*l:128*l+128]
    if vecs:
        b1_ref,b2_ref,gd_ref,gd0_ref,gf_ref=vecs
        for chip in range(2):
            cols=slice(128*chip,128*chip+128)
            half=jnp.where(i<2,b1_ref[:,cols],b2_ref[:,cols])
            line=lambda ref,k:ref[k:k+1,cols]
            ten=[jnp.zeros((2,128),f32),half,line(gd_ref,5),gd_ref[3:5,cols],gd_ref[1:3,cols],line(gd0_ref,0),line(gd_ref,6)]
            pick=lambda v,at:sum(jnp.where(i==k,gf_ref[4*v+k:4*v+k+1,at:at+128],0.0) for k in range(4))
            long=[pick(v,512*chip+128*b) for v in (2,0,1) for b in range(4)]
            rows=jnp.concatenate(ten+long+[jnp.zeros((1,128),f32)],axis=0).astype(bf16)
            for r in range(8):
                part=rows[8*r:8*r+8,:] if r<3 else jnp.zeros((8,128),bf16)
                keep_ref[r,chip,96:104,:]=part
                give_ref[r,chip,96:104,:]=part

def grad_qkv(core,a,dq,dk,dv,vecs=()):
    t,d=a.shape; w=dq.shape[1]; rows=104 if vecs else 96
    full=pl.BlockSpec((t,w),lambda i,c:(0,0),pipeline_mode=pl.Buffered(1))
    out=pl.BlockSpec((8,2,rows,128),lambda i,c:(0,i,0,0))
    lanes=lambda v:pl.BlockSpec((v.shape[0],256),lambda i,c:(0,i))
    more=[]
    if vecs:
        b1,b2,gd,gd0,gf=vecs
        half=lambda lo:pl.BlockSpec((2,256),lambda i,c:(0,jnp.clip(i-lo,0,1)))
        more=[half(0),half(2),lanes(gd),lanes(gd0),pl.BlockSpec(gf.shape,lambda i,c:(0,0))]
    return hbm_call(grad_qkv_kernel,
        grid_spec=pltpu.PrefetchScalarGridSpec(num_scalar_prefetch=1,grid=(4,),
            in_specs=[pl.BlockSpec((t,256),lambda i,c:(0,i)),full,full,full]+more,
            out_specs=[out,out]),
        out_shape=[pltpu.HBM((8,8,rows,128),bf16)]*2,
        compiler_params=pltpu.CompilerParams(vmem_limit_bytes=48<<20),name="grad_qkv",cost_estimate=cost(8))(core,a,dq,dk,dv,*vecs)

def totals_kernel(*refs):
    *parts,out_ref=refs
    at=0
    for p in parts:
        n=p.shape[1]
        total=jnp.sum(p[...].astype(f32),axis=0).astype(bf16)
        for r in range(8):
            out_ref[r,at:at+n,:]=total
        at+=n

def totals(parts):
    rows=sum(p.shape[1] for p in parts)
    return hbm_call(totals_kernel,out_shape=pltpu.HBM((8,rows,128),bf16),
        compiler_params=pltpu.CompilerParams(vmem_limit_bytes=40<<20),name="totals",cost_estimate=cost(4))(*parts)

def finish_kernel(core_ref,s_ref,qkv_ref,out_ref,fc1_ref,fc2_ref,ten_ref,three_ref):
    piece=lambda r,at,n:s_ref[r,at:at+n,:].astype(f32)
    for r in range(8):
        cols=slice(128*r,128*r+128)
        fc2_ref[:,cols]=piece(r,0,256)
        out_ref[:,cols]=piece(r,256,64)
        for j in range(4):
            fc1_ref[:,1024*j+128*r:1024*j+128*r+128]=piece(r,320+64*j,64)
    for half in range(2):
        for p in range(3):
            for l in range(4):
                lanes=1024*p+512*half+128*l
                for h in range(2):
                    q=2*(4*p+l)+h
                    qkv_ref[32*h:32*h+32,lanes:lanes+128]=piece(q//3,576+96*half+32*(q%3),32)
    first=core_ref[0]==0
    rows=jnp.concatenate([piece(r,768,8) for r in range(3)],axis=0)
    ten_ref[0:11,:]=jnp.where(first,rows[0:11,0:64],rows[0:11,64:128])
    ten_ref[11:16,:]=jnp.zeros((5,64),f32)
    for v in range(3):
        b=[rows[11+4*v+k:12+4*v+k,:] for k in range(4)]
        three_ref[v:v+1,0:128]=jnp.where(first,b[0],b[2])
        three_ref[v:v+1,128:256]=jnp.where(first,b[1],b[3])
    three_ref[3:8,:]=jnp.zeros((5,256),f32)

def finish(core,sums):
    sd=pltpu.HBM
    shapes=[(64,3072),(64,1024),(64,4096),(256,1024),(16,64),(8,256)]
    return hbm_call(finish_kernel,
        grid_spec=pltpu.PrefetchScalarGridSpec(num_scalar_prefetch=1,grid=(1,),
            in_specs=[pl.BlockSpec(sums.shape,lambda i,c:(0,0,0))],
            out_specs=[pl.BlockSpec(s,lambda i,c:(0,0)) for s in shapes]),
        out_shape=[sd(s,f32) for s in shapes],
        compiler_params=pltpu.CompilerParams(vmem_limit_bytes=40<<20),name="finish",cost_estimate=cost(5))(core,sums)

def pack_kernel(at_ref,*refs):
    *vecs,w_ref,out_ref=refs
    shard=at_ref[0]
    for j in range(3):
        out_ref[64*j:64*j+64,:]=w_ref[:,1024*j:1024*j+1024]
    lane=lax.broadcasted_iota(jnp.int32,(1,1024),1)
    rows=[]
    for r in vecs[:10]:
        v=r[...].astype(f32).reshape(1,-1)
        v=jnp.concatenate([v,v],axis=1)
        rows.append(jnp.where(lane//64==shard,jnp.concatenate([v]*8,axis=1),0.0))
    rows.append(jnp.where(lane//64==shard,jnp.broadcast_to(vecs[10][...].astype(f32).reshape(1,1),(1,1024)),0.0))
    for r in vecs[11:14]:
        v=jnp.concatenate([r[...].astype(f32).reshape(1,-1)]*4,axis=1)
        for j in range(4):
            rows.append(jnp.where(lane//256+4*j==shard,v,0.0))
    rows.append(jnp.zeros((1,1024),f32))
    out_ref[192:216,:]=jnp.concatenate(rows,axis=0).astype(bf16)

def pack_first(shard,vectors,w_qkv):
    full=lambda s:pl.BlockSpec(s,lambda i,c:(0,)*len(s))
    return hbm_call(pack_kernel,
        grid_spec=pltpu.PrefetchScalarGridSpec(num_scalar_prefetch=1,grid=(1,),
            in_specs=[full(v.shape) for v in vectors]+[full(w_qkv.shape)],out_specs=full((216,1024))),
        out_shape=pltpu.HBM((216,1024),bf16),name="pack_first",cost_estimate=cost(2))(shard,*vectors,w_qkv)

T=1152; D=1024
FWD_BLOCKS=[(0,384),(384,384),(768,384)]
BLOCKS=[(0,256),(256,256),(512,256),(768,256),(1024,128)]


def masked_scores(sT, start_row, q0, bq):
    keys=q0+bq
    kio=lax.broadcasted_iota(jnp.int32,(128,bq),0)
    qio=lax.broadcasted_iota(jnp.int32,(1,bq),1)+q0
    parts=[]
    for k0 in range(0,keys,128):
        t=sT[k0:k0+128]
        ok=None
        if k0==0 or q0+bq>1024:
            ok=kio>=start_row-k0
        if k0+127>q0:
            low=kio<=qio-k0
            ok=low if ok is None else ok&low
        parts.append(t if ok is None else jnp.where(ok,t,NEG))
    return jnp.concatenate(parts,axis=0) if len(parts)>1 else parts[0]

def fwd_kernel(start_ref,hs_ref,q_ref,k_ref,v_ref,o_ref,c_ref,lse_ref):
    lane=lax.broadcasted_iota(jnp.int32,(1,128),1)
    vT=v_ref[...].T
    oT=[]
    for q0,bq in FWD_BLOCKS:
        keys=q0+bq
        k=k_ref[0:keys,:]
        qb=q_ref[q0:q0+bq,:]*jnp.asarray(HD**-0.5,bf16)
        start=start_ref[0:1,q0:q0+bq]
        halves=[]
        for h in range(2):
            qh=jnp.where((lane>=64*h)&(lane<64*h+64),qb,jnp.zeros_like(qb))
            s=masked_scores(dot(k,qh,NT),start,q0,bq)
            m=jnp.max(s,axis=0,keepdims=True)
            e=jnp.exp(s-m)
            l=jnp.sum(e,axis=0,keepdims=True)
            lse_ref[0,h:h+1,q0:q0+bq]=m+jnp.log(l)
            oh=dot(vT[64*h:64*h+64,0:keys],e.astype(bf16))
            halves.append(oh*(1.0/l))
        o=jnp.concatenate(halves,axis=0).T
        o_ref[q0:q0+bq,:]=o
        c_ref[q0:q0+bq,:]=(o*hs_ref[10:11,:]).astype(bf16)

def attn_fwd(proj,start,hs_cols):
    return hbm_call(fwd_kernel,
        grid=(H//2,),
        in_specs=[pl.BlockSpec((1,T),lambda p:(0,0)),pl.BlockSpec((24,128),lambda p:(0,p)),
                  pl.BlockSpec((T,128),lambda p:(0,p)),pl.BlockSpec((T,128),lambda p:(0,8+p)),pl.BlockSpec((T,128),lambda p:(0,16+p))],
        out_specs=[pl.BlockSpec((T,128),lambda p:(0,p)),pl.BlockSpec((T,128),lambda p:(0,p)),pl.BlockSpec((1,2,T),lambda p:(p,0,0))],
        out_shape=[pltpu.HBM((T,D),f32),pltpu.HBM((T,D),bf16),pltpu.HBM((H//2,2,T),f32)],
        compiler_params=pltpu.CompilerParams(vmem_limit_bytes=48<<20),
        name="attn_fwd",cost_estimate=cost(40))(start,hs_cols,proj,proj,proj)

def bwd_kernel(start_ref,lse_ref,o_ref,q_ref,k_ref,v_ref,do_ref,dq_ref,dk_ref,dv_ref,bsum_ref,dk_acc,dv_acc,dqT):
    lane=lax.broadcasted_iota(jnp.int32,(1,128),1)
    scale=jnp.asarray(HD**-0.5,bf16)
    kT=(k_ref[...]*scale).T
    prodT=(o_ref[...]*do_ref[...].astype(f32)).T
    delta=[jnp.sum(prodT[64*h:64*h+64],axis=0,keepdims=True) for h in range(2)]
    dk_acc[...]=jnp.zeros_like(dk_acc)
    dv_acc[...]=jnp.zeros_like(dv_acc)
    for q0,bq in BLOCKS:
        keys=q0+bq
        k=k_ref[0:keys,:]
        v=v_ref[0:keys,:]
        qb=q_ref[q0:q0+bq,:]*scale
        dob=do_ref[q0:q0+bq,:]
        start=start_ref[0:1,q0:q0+bq]
        for h in range(2):
            half=(lane>=64*h)&(lane<64*h+64)
            qh=jnp.where(half,qb,jnp.zeros_like(qb))
            doh=jnp.where(half,dob,jnp.zeros_like(dob))
            s=masked_scores(dot(k,qh,NT),start,q0,bq)
            p=jnp.exp(s-lse_ref[0,h:h+1,q0:q0+bq])
            dp=dot(v,doh,NT)
            ds=(p*(dp-delta[h][:,q0:q0+bq])).astype(bf16)
            dv_acc[0:keys,:]+=dot(p.astype(bf16),doh)
            dk_acc[0:keys,:]+=dot(ds,qh)
            dqT[64*h:64*h+64,q0:q0+bq]=dot(kT[64*h:64*h+64,0:keys],ds)
    dq=dqT[...].T.astype(bf16)
    dk=dk_acc[...].astype(bf16)
    dv=dv_acc[...].astype(bf16)
    dq_ref[...]=dq; dk_ref[...]=dk; dv_ref[...]=dv
    bsum_ref[0:1,:]=jnp.sum(dq.astype(f32),axis=0,keepdims=True)
    bsum_ref[1:2,:]=jnp.sum(dv.astype(f32),axis=0,keepdims=True)

def attn_bwd(proj,start,lse,o,do,half):
    pairs=H//4; at=half*pairs
    blk=lambda off:pl.BlockSpec((T,128),lambda p:(0,off+at+p))
    out=pl.BlockSpec((T,128),lambda p:(0,p))
    return hbm_call(bwd_kernel,
        grid=(pairs,),
        in_specs=[pl.BlockSpec((1,T),lambda p:(0,0)),pl.BlockSpec((1,2,T),lambda p:(at+p,0,0)),blk(0),blk(0),blk(8),blk(16),blk(0)],
        out_specs=[out,out,out,pl.BlockSpec((2,128),lambda p:(0,p))],
        out_shape=[pltpu.HBM((T,D//2),bf16)]*3+[pltpu.HBM((2,D//2),f32)],
        scratch_shapes=[pltpu.VMEM((T,128),f32),pltpu.VMEM((T,128),f32),pltpu.VMEM((128,T),f32)],
        compiler_params=pltpu.CompilerParams(vmem_limit_bytes=48<<20),
        name="attn_bwd",cost_estimate=cost(20))(start,lse,o,proj,proj,proj,do)

EVERY = ("replica", "chip", "core")
SHARD = ("chip", "core")
PEERS = ("replica", "chip")


def exchange(slab, devices):
    return lax.all_to_all(slab.reshape(devices, -1, 128), EVERY, split_axis=0, concat_axis=0, tiled=True).reshape(-1, 128)


def replica_parts(part):
    return lax.all_to_all(part, "replica", split_axis=0, concat_axis=0, tiled=True)


def core_sum(keep, give):
    taken = lax.ppermute(give, "core", [(0, 1), (1, 0)])
    both = keep.astype(f32) + taken.astype(f32)
    return both.astype(bf16).reshape(64, *keep.shape[2:])


def peer_parts(both):
    return lax.all_to_all(both, PEERS, split_axis=0, concat_axis=0, tiled=True)


def on_device(
    tokens, cotangent, lengths, deal_order, inverse, ln1_gain, ln1_bias, w_qkv, b_query, b_value, head_scale, w_out, b_out,
    post_gain, post_bias, ln2_gain, ln2_bias, w_fc1, b_fc1, ffn_gain, ffn_bias, w_fc2, b_fc2,
):
    devices = lax.axis_size(EVERY)
    replicas = lax.axis_size("replica")
    count, width = tokens.shape
    core = lax.axis_index("core").astype(jnp.int32).reshape(1)
    shard = lax.axis_index(SHARD).astype(jnp.int32).reshape(1)
    vectors = [ln1_gain, ln1_bias, b_query, b_value, b_out, post_gain, post_bias, ln2_gain, ln2_bias, b_fc2, head_scale,
               b_fc1, ffn_gain, ffn_bias]
    first = pack_first(shard, vectors, w_qkv)
    pack1 = lax.all_gather(first, SHARD, axis=0)
    recv_keys = deal_order // count * count + jnp.arange(count, dtype=jnp.int32)
    first, tokens = lax.optimization_barrier((first, tokens))
    sent_x = send_rows(tokens, inverse)
    got_x = exchange(sent_x, devices)
    sent_x, w_out, w_fc1, cotangent = lax.optimization_barrier((sent_x, w_out, w_fc1, cotangent))
    packa = lax.all_gather(jnp.concatenate([w_out] + [w_fc1[:, width * j : width * j + width] for j in range(4)], axis=0), SHARD, axis=0)
    packb = lax.all_gather(w_fc2, SHARD, axis=0)
    sent_dy = send_rows(cotangent, inverse)
    sent_dy, got_x, pack1 = lax.optimization_barrier((sent_dy, got_x, pack1))
    got_dy = exchange(sent_dy, devices)
    vec = jnp.sum(pack1[:, 192:216].astype(f32), axis=0)
    places = jnp.arange(count, dtype=jnp.int32)
    starts = jnp.zeros((count,), jnp.int32)
    seq_end = jnp.zeros((), jnp.int32)
    for i in range(lengths.shape[1]):
        seq_end = seq_end + lengths[0, i]
        starts = jnp.where(places >= seq_end, seq_end, starts)
    starts = starts.reshape(1, count)
    x_rows, a, proj = recv_qkv(got_x, recv_keys, vec, pack1)
    o, c, lse = attn_fwd(proj, starts, vec)
    got_dy, c = lax.optimization_barrier((got_dy, c))
    dy_rows = recv_rows(got_dy, recv_keys)
    a2, n, vhat, gp, hres, zhat, stats = up_rows(c, x_rows, vec, packa)
    grads_fc2 = grad_fc2(n, dy_rows)
    grads_fc2, gp = lax.optimization_barrier((grads_fc2, gp))
    part_fc2 = lax.psum_scatter(grads_fc2, SHARD, scatter_dimension=0)
    sent_y, du, gd0, gf = down_rows(n, vhat, gp, stats, dy_rows, hres, vec, packb, recv_keys)
    sent_y, du = lax.optimization_barrier((sent_y, du))
    got_y = exchange(sent_y, devices)
    dz, do, dres, gd = back_rows(du, dy_rows, hres, zhat, stats, o, vec, packa)
    grads_up = grad_up(c, dz, a2, du)
    grads_up, do, got_y = lax.optimization_barrier((grads_up, do, got_y))
    part_up = lax.psum_scatter(grads_up, SHARD, scatter_dimension=0)
    halves1 = attn_bwd(proj, starts, lse, o, do, 0)
    dq1, part_fc2 = lax.optimization_barrier((halves1[0], part_fc2))
    parts_fc2 = replica_parts(part_fc2)
    both1 = core_sum(*grad_qkv(core, a, dq1, *halves1[1:3]))
    both1, do, parts_fc2 = lax.optimization_barrier((both1, do, parts_fc2))
    parts1 = peer_parts(both1)
    halves2 = attn_bwd(proj, starts, lse, o, do, 1)
    dq2, parts1 = lax.optimization_barrier((halves2[0], parts1))
    keep2, give2 = grad_qkv(core, a, dq2, *halves2[1:3], (halves1[3], halves2[3], gd, gd0, gf))
    keep2, give2, part_up = lax.optimization_barrier((keep2, give2, part_up))
    parts_up = replica_parts(part_up)
    both2 = core_sum(keep2, give2)
    both2, parts_up = lax.optimization_barrier((both2, parts_up))
    parts2 = peer_parts(both2)
    both2, dq2 = lax.optimization_barrier((both2, dq2))
    sent_dx = dx_send([dq1, *halves1[1:3], dq2, *halves2[1:3]], x_rows, dres, vec, pack1, recv_keys)
    sent_dx, parts2 = lax.optimization_barrier((sent_dx, parts2))
    got_dx = lax.all_to_all(sent_dx, EVERY, split_axis=0, concat_axis=0, tiled=True)
    parts_up, got_y, sent_dx = lax.optimization_barrier((parts_up, got_y, sent_dx))
    output = recv_rows(got_y, inverse)
    spread = totals([parts_fc2, parts_up, parts1, parts2])
    spread, got_dx, output = lax.optimization_barrier((spread, got_dx, output))
    sums = lax.all_to_all(spread, "replica", split_axis=0, concat_axis=0, tiled=True)
    grad_tokens, g_ln1 = recv_more(got_dx, inverse)
    g_ln1 = jnp.where(core[0] == 0, g_ln1[0:2, 0:64], g_ln1[0:2, 64:128])
    g_qkv, g_out, g_fc1, g_fc2, ten, three = finish(core, sums)
    v = [ten[k] for k in range(10)]
    return (
        output, grad_tokens, g_ln1[0], g_ln1[1], g_qkv, v[2], v[3], jnp.sum(ten[10]).reshape(1), g_out, v[4], v[5], v[6], v[7], v[8], g_fc1,
        three[0], three[1], three[2], g_fc2, v[9],
    )


def solution(mesh):
    replicas, shards = mesh.devices.shape
    mesh = jax.sharding.Mesh(mesh.devices.reshape(replicas, shards // 2, 2), EVERY)
    rows, vector, matrix = P(EVERY, None), P(SHARD), P(SHARD, None)
    in_specs = (
        rows, rows, rows, P(EVERY), P(EVERY), vector, vector, matrix, vector, vector, vector, matrix, vector, vector, vector,
        vector, vector, matrix, vector, vector, vector, matrix, vector,
    )
    out_specs = (
        rows, rows, vector, vector, matrix, vector, vector, vector, matrix, vector, vector, vector, vector, vector, matrix,
        vector, vector, vector, matrix, vector,
    )
    return jax.shard_map(on_device, mesh=mesh, in_specs=in_specs, out_specs=out_specs, check_vma=False)
```
